512 devices in a mesh: rows: 32 (over z, core), cols: 16 (over x, y).
Axes of the slice: x: 4, y: 4, z: 16, core: 2. Of those that a mesh axis runs over, the one named last changes fastest.
Arguments:
- matrix: float32 [131072, 4096], P('rows', 'cols'), may hold values from -80 to 80
- mixers: float32 [8, 128, 128], replicated, may hold values from -0.0009765625 to 0.0009765625
- bucket_pair: int32 [1024, 2], P('rows'), may hold values from 0 to 63, all different within a row; in each aligned block of 32 rows (0 to 31, 32 to 63, ...) at most 2 rows name the same one
- mixer_index: int32 [1024], P('rows'), may hold values from 0 to 7
- sign_seed: int32 [1024], P('rows'), may hold values from 0 to 1073741823
Outputs:
- projected: float32 [256, 4096], P('rows', 'cols')
The draws below stay inside these ranges and needn't reach their ends.
Inputs may be any that keep to these rules, and one draw needn't show every extreme that they name: `bucket_pair`: the two buckets of a tile differ; among the 32 tiles of one device no bucket is named more than 2 times, a bound that some block reaches.
All inputs are finite; a program needn't handle non-finite values.
Results may differ from the reference program's by a relative error of at most 0.0012.
Values may be sent and summed in bfloat16 or wider, within the bound.
A program may use at most 64 MiB of HBM per device.

```python
import math
import jax
import jax.numpy as jnp
import numpy as np
from jax import lax

NCOL = 4096
SKETCH = 8192
TILE = 128
P_SIZE = 256
MIXERS = 8
MOST = 2
TILES_DEV = 32
NB = 64
NT = 1024
ROWS_ALL = 131072


def draw_matrix(key, part):
    base_key = jax.random.fold_in(key, 11)
    first_key = jax.random.fold_in(base_key, 0)
    base = jax.random.normal(first_key, (ROWS_ALL, NCOL), jnp.float32)
    echo = jnp.tile(base[:, :P_SIZE], (1, NCOL // P_SIZE))
    column = jnp.arange(NCOL, dtype=jnp.int32)
    keep_mask = (column >= P_SIZE).astype(jnp.float32)
    result = base + 0.8 * echo * keep_mask[None, :]
    return jnp.clip(result, -80.0, 80.0)


def set_ends(array, rng, smallest, largest):
    longest = array.shape.index(max(array.shape))
    spots = []
    for shift in (0, 1):
        where = [jax.random.randint(jax.random.fold_in(rng, axis), (), 0, length) for axis, length in enumerate(array.shape)]
        where[longest] = (where[longest] + shift) % array.shape[longest]
        spots.append(tuple(where))
    return array.at[spots[0]].set(smallest).at[spots[1]].set(largest)


def shared_out(key, own, number, rows, amount, top, bound, skew):
    order = jax.random.permutation(key, amount)
    crowded, usual = portions_of(amount, rows * top, bound, skew, True), portions_of(amount, rows * top, bound, skew, False)
    places = jnp.arange(amount)

    def named(lengths, rotation):
        used = int((lengths > 0).sum())
        fixed = max(1, used // 4)
        passed = fixed + (places - fixed + rotation * (used - fixed)) % max(1, amount - fixed)
        return jnp.zeros((amount,), jnp.int32).at[order[jnp.where(places < fixed, places, passed)]].set(jnp.asarray(lengths, jnp.int32))

    lengths = jnp.where(number % 4 == 0, named(crowded, number // 4), named(usual, number - number // 4 - 1))
    mixed = jax.random.permutation(jax.random.fold_in(own, 3), amount)
    source_of, receiver = mixed[0:amount // 2 * 2:2], mixed[1:amount // 2 * 2:2]
    margin = jnp.minimum(lengths[source_of] - 1, bound - lengths[receiver]) // 2
    margin = jnp.where((source_of == order[0]) | (receiver == order[0]) | (lengths[receiver] == 0), 0, jnp.maximum(margin, 0))
    passed = jax.random.randint(jax.random.fold_in(own, 4), (amount // 2,), 0, 1 << 20) % (margin + 1)
    lengths = lengths.at[source_of].add(-passed).at[receiver].add(passed)
    items = jnp.searchsorted(jnp.cumsum(lengths), jnp.arange(rows * top), side="right").astype(jnp.int32)
    listing = items.reshape(top, rows).T
    listing = listing[jax.random.permutation(jax.random.fold_in(own, 1), rows)]
    rotation = jax.random.randint(jax.random.fold_in(own, 2), (rows, 1), 0, top)
    return jnp.take_along_axis(listing, (jnp.arange(top)[None, :] + rotation) % top, axis=1)


def portions_of(count, total, limit, skew, full):
    portions = [(1 << 20) // math.isqrt(standing ** skew) + 1 for standing in range(1, count + 1)]
    largest = limit if full else min(limit, max(-(-total // count), total * portions[0] // sum(portions)))
    least = 1 if total - largest >= count - 1 else 0
    given, spare = [largest] + [least] * (count - 1), total - largest - least * (count - 1)
    while spare > 0:
        free = [i for i in range(1, count) if given[i] < largest] or [i for i in range(1, count) if given[i] < limit]
        mass, remaining = sum([portions[i] for i in free]), spare
        for i in free:
            extra = min(limit - given[i], max(1, remaining * portions[i] // mass), spare)
            given[i] = given[i] + extra
            spare = spare - extra
    return np.array(given)


def bell_draw(key, dims, spread, reach, held_as=jnp.bfloat16):
    return jnp.clip(spread * jax.random.normal(key, dims, jnp.float32), -reach, reach).astype(held_as)


def setup_inputs(seed: int = 0) -> dict:
    key_of = jax.random.split(jax.random.key(seed), 6)
    matrix = draw_matrix(jax.random.fold_in(key_of[5], 71), 0)
    mixers = bell_draw(key_of[1], (MIXERS, TILE, TILE), (TILE * TILE * 2 * NT) ** -0.5, 0.0009765625, jnp.float32)
    bucket_pair_keys = jax.random.split(jax.random.fold_in(key_of[2], 1), NT // TILES_DEV)
    bucket_pair_turns = jax.random.permutation(jax.random.fold_in(key_of[2], 3), NT // TILES_DEV)
    bucket_pair = jax.vmap(lambda own, number: shared_out(jax.random.fold_in(key_of[2], 2), own, number, TILES_DEV, NB, 2, MOST, 2))(bucket_pair_keys, bucket_pair_turns).reshape((NT, 2))
    mixer_index = set_ends(jax.random.randint(key_of[3], (NT,), 0, MIXERS), jax.random.fold_in(key_of[3], 1), 0, MIXERS - 1).astype(jnp.int32)
    sign_seed = set_ends(jax.random.randint(key_of[4], (NT,), 0, 1073741824), jax.random.fold_in(key_of[4], 1), 0, 1073741823).astype(jnp.int32)
    return dict(matrix=matrix, mixers=mixers, bucket_pair=bucket_pair, mixer_index=mixer_index, sign_seed=sign_seed)


def row_signs(seed_vals):
    position = jnp.arange(TILE, dtype=jnp.int32)
    hashed = (seed_vals[:, None] ^ position[None, :] * 40503) * 69069
    hashed_bit = hashed >> 16 & 1
    return (1 - 2 * hashed_bit).astype(jnp.float32)

def tile_flips(seed_vals):
    return (1 - 2 * (seed_vals >> 29 & 1)).astype(jnp.float32)

def reference(matrix, mixers, bucket_pair, mixer_index, sign_seed):
    blocks = matrix.reshape(NT, TILE, NCOL)
    row_sign = row_signs(sign_seed)
    tile_flip = tile_flips(sign_seed)

    def add_tile(totals, per_tile):
        block, signs_here, which, pair, flip = per_tile
        mixed_tile = jnp.dot(mixers[which].astype(jnp.float32), (signs_here[:, None] * block).astype(jnp.float32), precision=lax.Precision.HIGHEST, preferred_element_type=jnp.float32).astype(jnp.bfloat16)
        widened = mixed_tile.astype(jnp.float32)
        totals = totals.at[pair[0]].add(widened)
        totals = totals.at[pair[1]].add(flip * widened)
        return (totals, None)
    start = jnp.zeros((NB, TILE, NCOL), jnp.float32)
    totals, unused = lax.scan(add_tile, start, (blocks, row_sign, mixer_index, bucket_pair, tile_flip))
    sketch = totals.reshape(SKETCH, NCOL)
    panel_cols = sketch[:, :P_SIZE]
    gram_total = jnp.dot(panel_cols.T.astype(jnp.float32), panel_cols.astype(jnp.float32), precision=lax.Precision.HIGHEST, preferred_element_type=jnp.float32)
    factor = jnp.linalg.cholesky(gram_total)
    basis_rows = lax.linalg.triangular_solve(factor, panel_cols.T, left_side=True, lower=True).T
    return jnp.dot(basis_rows.T.astype(jnp.float32), sketch.astype(jnp.float32), precision=lax.Precision.HIGHEST, preferred_element_type=jnp.float32)
```

```python
import functools

import jax
import jax.numpy as jnp
from jax import lax
from jax.experimental import pallas as pl
from jax.experimental.pallas import tpu as pltpu
from jax.sharding import Mesh
from jax.sharding import PartitionSpec as P

TILE = 128
PS = 256
NB = 64
TD = 32
NZ = 16
NK = 2
NX = 4
NC = 16
G = 8
HALF = 128
MESH = pl.DeviceIdType.MESH
HI = lax.Precision.HIGHEST
ROWS = ("z", "k")
COLS = ("x", "y")
F32 = jnp.float32
BF16 = jnp.bfloat16


def place():
    return tuple(lax.axis_index(a) for a in ("z", "k", "x", "y"))


def remote(src, dst, send, recv, to):
    return pltpu.make_async_remote_copy(
        src_ref=src, dst_ref=dst, send_sem=send, recv_sem=recv, device_id=to, device_id_type=MESH
    )


def hello(to):
    pl.semaphore_signal(pltpu.get_barrier_semaphore(), inc=1, device_id=to, device_id_type=MESH)


def meet(count):
    pl.semaphore_wait(pltpu.get_barrier_semaphore(), count)


STEP_TILES = 8


def mix_kernel(which, seeds, mat, mixers, out):
    step = pl.program_id(0)
    lane = lax.broadcasted_iota(jnp.int32, (1, TILE), 1) * 40503
    for pair in range(STEP_TILES // 2):
        parts = []
        for q in range(2):
            here = 2 * pair + q
            tile = step * STEP_TILES + here
            hashed = (seeds[tile] ^ lane) * 69069
            sign = (1 - 2 * ((hashed >> 16) & 1)).astype(F32)
            mixer = mixers[which[tile]] * sign
            block = mat[here * TILE : (here + 1) * TILE, :]
            mixed = jnp.dot(mixer, block, precision=HI, preferred_element_type=F32)
            parts.append(mixed.reshape(TILE // G, G, mixed.shape[1]))
        out[:, pair * 2 * G : (pair + 1) * 2 * G, :] = jnp.concatenate(parts, axis=1).astype(BF16)


def mix(which, seeds, matrix, mixers):
    width = matrix.shape[1]
    return pl.pallas_call(
        mix_kernel,
        out_shape=jax.ShapeDtypeStruct((TILE // G, TD * G, width), BF16),
        grid_spec=pltpu.PrefetchScalarGridSpec(
            num_scalar_prefetch=2,
            grid=(TD // STEP_TILES,),
            in_specs=[
                pl.BlockSpec((STEP_TILES * TILE, width), lambda i, a, b: (i, 0)),
                pl.BlockSpec(mixers.shape, lambda i, a, b: (0, 0, 0)),
            ],
            out_specs=pl.BlockSpec((TILE // G, STEP_TILES * G, width), lambda i, a, b: (0, i, 0)),
        ),
        name="mix",
    )(which, seeds, matrix, mixers)


def scatter_kernel(m_ref, sel_ref, x_ref, other_ref, send, recv, local, sel_sems):
    z, k, x, y = place()
    col = x * NX + y
    source = col == 0
    sibling = {"k": 1 - k}
    hello(sibling)
    for ks in range(NK):
        @pl.when(jnp.logical_not(source))
        def _():
            hello({"k": ks, "x": 0, "y": 0})

    @pl.when(source)
    def _():
        meet(NK * NC - 1)

    @pl.when(jnp.logical_not(source))
    def _():
        meet(1)

    swap = remote(sel_ref, other_ref, sel_sems.at[0], sel_sems.at[1], sibling)
    swap.start()

    def piece(c, kd):
        part = m_ref.at[c, :, pl.ds(pl.multiple_of(kd * HALF, HALF), HALF)]
        return remote(
            part, x_ref.at[k], send.at[c, kd], recv.at[k], {"k": kd, "x": c // NX, "y": c % NX}
        )

    own = pltpu.make_async_copy(
        m_ref.at[0, :, pl.ds(pl.multiple_of(k * HALF, HALF), HALF)], x_ref.at[k], local
    )

    @pl.when(source)
    def _():
        for c in range(1, NC):
            for kd in range(NK):
                piece(c, kd).start()
        piece(0, 1 - k).start()
        own.start()
        own.wait()
        for c in range(1, NC):
            for kd in range(NK):
                piece(c, kd).wait_send()
        piece(0, 1 - k).wait_send()
        remote(x_ref.at[1 - k], x_ref.at[1 - k], send.at[0, 0], recv.at[1 - k], sibling).wait_recv()

    @pl.when(jnp.logical_not(source))
    def _():
        for ks in range(NK):
            remote(x_ref.at[ks], x_ref.at[ks], send.at[0, 0], recv.at[ks], sibling).wait_recv()

    swap.wait()


ANY = pl.BlockSpec(memory_space=pl.ANY)
VM = pl.BlockSpec(memory_space=pltpu.VMEM)
DMA = pltpu.SemaphoreType.DMA


def scatter(mixed, sel):
    return pl.pallas_call(
        scatter_kernel,
        out_shape=(
            jax.ShapeDtypeStruct((NK, TD * G, HALF), BF16),
            jax.ShapeDtypeStruct(sel.shape, BF16),
        ),
        in_specs=[ANY, ANY],
        out_specs=(ANY, ANY),
        scratch_shapes=[DMA((NC, NK)), DMA((NK,)), DMA, DMA((2,))],
        compiler_params=pltpu.CompilerParams(collective_id=1, has_side_effects=True),
        name="scatter",
    )(mixed, sel)


def total_kernel(y_ref, p_ref, got, send_a, recv_a, send_b, recv_b, send_c, recv_c):
    z, k, x, y = place()
    sibling = {"k": 1 - k}
    hello(sibling)
    for d in range(1, NZ):
        hello({"z": lax.rem(z + d, NZ)})
    meet(NZ)
    for d in range(1, NZ):
        zt = lax.rem(z + d, NZ)
        remote(y_ref.at[zt], got.at[d - 1], send_a.at[d - 1], recv_a.at[d - 1], {"z": zt}).start()
    acc = y_ref[z]
    for d in range(1, NZ):
        remote(got.at[d - 1], got.at[d - 1], send_a.at[d - 1], recv_a.at[d - 1], sibling).wait_recv()
        acc = acc + got[d - 1]
    p_ref[k, z] = acc
    for d in range(1, NZ):
        zt = lax.rem(z + d, NZ)
        remote(p_ref.at[k, z], p_ref.at[k, z], send_b.at[d - 1], recv_b.at[d - 1], {"z": zt}).start()

    def hand(d):
        zs = lax.rem(z + NZ - d, NZ)
        return remote(p_ref.at[k, zs], p_ref.at[k, zs], send_c.at[d], recv_c.at[d], sibling)

    hand(0).start()
    for d in range(1, NZ):
        zs = lax.rem(z + NZ - d, NZ)
        remote(p_ref.at[k, zs], p_ref.at[k, zs], send_b.at[d - 1], recv_b.at[d - 1], sibling).wait_recv()
        hand(d).start()
    for d in range(NZ):
        zs = lax.rem(z + NZ - d, NZ)
        remote(
            p_ref.at[1 - k, zs], p_ref.at[1 - k, zs], send_c.at[d], recv_c.at[d], sibling
        ).wait_recv()
    for d in range(1, NZ):
        remote(got.at[d - 1], got.at[d - 1], send_a.at[d - 1], recv_a.at[d - 1], sibling).wait_send()
        remote(p_ref.at[k, z], p_ref.at[k, z], send_b.at[d - 1], recv_b.at[d - 1], sibling).wait_send()
    for d in range(NZ):
        hand(d).wait_send()


def total(part):
    rows = part.shape[0] // NZ
    return pl.pallas_call(
        total_kernel,
        out_shape=jax.ShapeDtypeStruct((NK, NZ, rows, HALF), F32),
        in_specs=[VM],
        out_specs=VM,
        scratch_shapes=[
            pltpu.VMEM((NZ - 1, rows, HALF), F32),
            DMA((NZ - 1,)),
            DMA((NZ - 1,)),
            DMA((NZ - 1,)),
            DMA((NZ - 1,)),
            DMA((NZ,)),
            DMA((NZ,)),
        ],
        compiler_params=pltpu.CompilerParams(collective_id=2, has_side_effects=True),
        name="total",
    )(part.reshape(NZ, rows, HALF))


def share_kernel(w_ref, g_ref, all_ref, gram_ref, got, send_w, recv_w, send_g, recv_g, send_h, recv_h, local):
    z, k, x, y = place()
    col = x * NX + y
    row = z * NK + k
    for c in range(1, NC):
        other = lax.rem(col + c, NC)
        hello({"x": other // NX, "y": lax.rem(other, NX)})
    for d in range(1, NZ * NK):
        other = lax.rem(row + d, NZ * NK)
        hello({"z": other // NK, "k": lax.rem(other, NK)})
    meet(NC - 1 + NZ * NK - 1)

    quarter = PS // 4

    def slot(h, c, s):
        return all_ref.at[c, pl.ds((2 * h + s) * quarter, quarter), :]

    def to(h, stage, direction):
        along_x = (h == 0) == (stage == 0)
        step = 1 if direction == 0 else NX - 1
        if along_x:
            return {"x": lax.rem(x + step, NX)}
        return {"y": lax.rem(y + step, NX)}

    def index(h, a, b):
        if h == 0:
            return lax.rem(x + a, NX) * NX + lax.rem(y + b, NX)
        return lax.rem(x + b, NX) * NX + lax.rem(y + a, NX)

    def move(h, a, b, s, stage, direction, first=None):
        c = index(h, a, b)
        src = slot(h, c, s) if first is None else first
        return remote(src, slot(h, c, s), send_w.at[h, c, s, stage, direction], recv_w.at[h, c, s], to(h, stage, direction))

    def arrived(h, a, b, s):
        c = index(h, a, b)
        remote(
            slot(h, c, s), slot(h, c, s), send_w.at[h, c, s, 0, 0], recv_w.at[h, c, s], {"k": 1 - k}
        ).wait_recv()

    sent = []

    def go(copy):
        copy.start()
        sent.append(copy)

    keep = pltpu.make_async_copy(w_ref, all_ref.at[col], local)
    keep.start()

    own = lambda h, s: w_ref.at[pl.ds((2 * h + s) * quarter, quarter), :]
    for s in range(2):
        for h in range(2):
            go(move(h, 0, 0, s, 0, s, own(h, s)))
    for s in range(2):
        for h in range(2):
            go(move(h, 0, 0, s, 0, 1 - s, own(h, s)))
    grow = pl.multiple_of(row * G, G)
    for c in range(1, NC):
        other = lax.rem(col + c, NC)
        go(
            remote(
                g_ref.at[pl.ds(grow, G), :],
                got.at[c - 1],
                send_g.at[c - 1],
                recv_g.at[c - 1],
                {"x": other // NX, "y": lax.rem(other, NX)},
            )
        )
    for s in range(2):
        for h in range(2):
            go(move(h, 0, 0, s, 1, s, own(h, s)))
    for s in range(2):
        for h in range(2):
            go(move(h, 0, 0, s, 1, 1 - s, own(h, s)))
    for h in range(2):
        arrived(h, 3, 0, 0)
        go(move(h, 3, 0, 0, 0, 0))
        arrived(h, 1, 0, 1)
        go(move(h, 1, 0, 1, 0, 1))
    for h in range(2):
        for a, s in ((3, 0), (1, 1)):
            go(move(h, a, 0, s, 1, s))
            go(move(h, a, 0, s, 1, 1 - s))
    for h in range(2):
        for a, s in ((3, 1), (1, 0)):
            arrived(h, a, 0, s)
            go(move(h, a, 0, s, 1, s))
            go(move(h, a, 0, s, 1, 1 - s))

    acc = g_ref[pl.ds(grow, G), :]
    for c in range(1, NC):
        remote(got.at[c - 1], got.at[c - 1], send_g.at[c - 1], recv_g.at[c - 1], {"k": 1 - k}).wait_recv()
        acc = acc + got[c - 1]
    gram_ref[pl.ds(grow, G), :] = acc
    mine = gram_ref.at[pl.ds(grow, G), :]
    for d in range(1, NZ * NK):
        other = lax.rem(row + d, NZ * NK)
        go(remote(mine, mine, send_h.at[d - 1], recv_h.at[d - 1], {"z": other // NK, "k": lax.rem(other, NK)}))

    for h in range(2):
        for s in range(2):
            arrived(h, 2, 0, s)
            go(move(h, 2, 0, s, 1, s))
            go(move(h, 2, 0, s, 1, 1 - s))
    for a in (0, 3, 1, 2):
        for h in range(2):
            arrived(h, a, 3, 0)
            go(move(h, a, 3, 0, 1, 0))
            arrived(h, a, 1, 1)
            go(move(h, a, 1, 1, 1, 1))
    for h in range(2):
        for a in (0, 3, 1, 2):
            arrived(h, a, 3, 1)
            arrived(h, a, 1, 0)
            for s in range(2):
                arrived(h, a, 2, s)
    for d in range(1, NZ * NK):
        other = lax.rem(row + NZ * NK - d, NZ * NK)
        theirs = gram_ref.at[pl.ds(pl.multiple_of(other * G, G), G), :]
        remote(theirs, theirs, send_h.at[d - 1], recv_h.at[d - 1], {"k": 1 - k}).wait_recv()
    for copy in sent:
        copy.wait_send()
    keep.wait()


def share(block, gram):
    return pl.pallas_call(
        share_kernel,
        out_shape=(
            jax.ShapeDtypeStruct((NC,) + block.shape, F32),
            jax.ShapeDtypeStruct(gram.shape, F32),
        ),
        in_specs=[VM, VM],
        out_specs=(VM, VM),
        scratch_shapes=[
            pltpu.VMEM((NC - 1, G, PS), F32),
            DMA((2, NC, 2, 2, 2)),
            DMA((2, NC, 2)),
            DMA((NC - 1,)),
            DMA((NC - 1,)),
            DMA((NZ * NK - 1,)),
            DMA((NZ * NK - 1,)),
            DMA,
        ],
        compiler_params=pltpu.CompilerParams(collective_id=3, has_side_effects=True),
        name="share",
    )(block, gram)


def finish_kernel(v_ref, o_ref, got, send, recv):
    z, k, x, y = place()
    row = z * NK + k
    parts = NZ * NK
    for d in range(1, parts):
        other = lax.rem(row + d, parts)
        hello({"z": other // NK, "k": lax.rem(other, NK)})
    meet(parts - 1)

    def copy(d):
        other = lax.rem(row + d, parts)
        return remote(
            v_ref.at[pl.ds(pl.multiple_of(other * G, G), G), :],
            got.at[d - 1],
            send.at[d - 1],
            recv.at[d - 1],
            {"z": other // NK, "k": lax.rem(other, NK)},
        )

    for d in range(1, parts):
        copy(d).start()
    acc = v_ref[pl.ds(pl.multiple_of(row * G, G), G), :]
    for d in range(1, parts):
        copy(d).wait_recv()
        acc = acc + got[d - 1]
    o_ref[...] = acc
    for d in range(1, parts):
        copy(d).wait_send()


def finish(value):
    parts = NZ * NK
    return pl.pallas_call(
        finish_kernel,
        out_shape=jax.ShapeDtypeStruct((G, value.shape[1]), F32),
        in_specs=[VM],
        out_specs=VM,
        scratch_shapes=[pltpu.VMEM((parts - 1, G, value.shape[1]), F32), DMA((parts - 1,)), DMA((parts - 1,))],
        compiler_params=pltpu.CompilerParams(collective_id=4, has_side_effects=True),
        name="finish",
    )(value)


def spread(sel):
    eye = jnp.eye(G, dtype=BF16)
    return (sel[:, None, :, None] * eye[None, :, None, :]).reshape(NB * G, TD * G)


def local(matrix, mixers, bucket_pair, mixer_index, sign_seed):
    mixed = mix(mixer_index, sign_seed, matrix, mixers)
    flip = (1 - 2 * (sign_seed >> 29 & 1)).astype(F32)
    bucket = jnp.arange(NB, dtype=jnp.int32)[:, None]
    sel = (bucket == bucket_pair[:, 0]).astype(F32) + flip * (bucket == bucket_pair[:, 1]).astype(F32)
    sel = sel.astype(BF16)
    panel, other = scatter(mixed, jnp.pad(sel, ((0, 0), (0, HALF - TD))))
    core = lax.axis_index("k")
    mine = spread(sel)
    theirs = spread(other[:, :TD])
    both = jnp.where(core == 0, jnp.concatenate([mine, theirs], 1), jnp.concatenate([theirs, mine], 1))
    part = jnp.dot(both, panel.reshape(NK * TD * G, HALF), preferred_element_type=F32)
    sketch = total(part).reshape(NK, NB * G, HALF)
    sketch = jnp.concatenate([sketch[0], sketch[1]], axis=1)
    weight = jnp.dot(mine.T.astype(F32), sketch, precision=HI, preferred_element_type=F32)
    gram_part = jnp.dot(sketch.T, sketch, precision=HI, preferred_element_type=F32)
    weights, gram = share(weight, gram_part)
    cross = jnp.dot(
        weights.reshape(NC * TD * G, PS).T,
        mixed.reshape(NC * TD * G, PS).astype(F32),
        precision=HI,
        preferred_element_type=F32,
    )
    factor = jnp.linalg.cholesky(gram)
    solved = lax.linalg.triangular_solve(factor, cross, left_side=True, lower=True)
    return finish(solved)


def solution(mesh):
    split = Mesh(mesh.devices.reshape(NZ, NK, NX, NX), ("z", "k", "x", "y"))
    return jax.shard_map(
        local,
        mesh=split,
        in_specs=(P(ROWS, COLS), P(), P(ROWS, None), P(ROWS), P(ROWS)),
        out_specs=P(ROWS, COLS),
        check_vma=False,
    )
```

```python
import functools

import jax
import jax.numpy as jnp
from jax import lax
from jax.experimental import pallas as pl
from jax.experimental.pallas import tpu as pltpu
from jax.sharding import Mesh
from jax.sharding import PartitionSpec as P

TILE = 128
PS = 256
NB = 64
TD = 32
NZ = 16
NK = 2
NX = 4
NC = 16
G = 8
HALF = 128
MESH = pl.DeviceIdType.MESH
HI = lax.Precision.HIGHEST
ROWS = ("z", "k")
COLS = ("x", "y")
F32 = jnp.float32
BF16 = jnp.bfloat16


def place():
    return tuple(lax.axis_index(a) for a in ("z", "k", "x", "y"))


def remote(src, dst, send, recv, to):
    return pltpu.make_async_remote_copy(
        src_ref=src, dst_ref=dst, send_sem=send, recv_sem=recv, device_id=to, device_id_type=MESH
    )


def hello(to):
    pl.semaphore_signal(pltpu.get_barrier_semaphore(), inc=1, device_id=to, device_id_type=MESH)


def meet(count):
    pl.semaphore_wait(pltpu.get_barrier_semaphore(), count)


def dot(a, b):
    return jnp.dot(a, b, precision=HI, preferred_element_type=F32)


STEP_TILES = 8


def mix_kernel(which, seeds, pairs, mat, mixers, out, meta):
    step = pl.program_id(0)
    lane = lax.broadcasted_iota(jnp.int32, (1, TILE), 1) * 40503
    for pair in range(STEP_TILES // 2):
        parts = []
        for q in range(2):
            here = 2 * pair + q
            tile = step * STEP_TILES + here
            hashed = (seeds[tile] ^ lane) * 69069
            sign = (1 - 2 * ((hashed >> 16) & 1)).astype(F32)
            mixer = mixers[which[tile]] * sign
            block = mat[here * TILE : (here + 1) * TILE, :]
            mixed = jnp.dot(mixer, block, precision=HI, preferred_element_type=F32)
            parts.append(mixed.reshape(TILE // G, G, mixed.shape[1]))
        out[:, pair * 2 * G : (pair + 1) * 2 * G, :] = jnp.concatenate(parts, axis=1).astype(BF16)

    @pl.when(step == 0)
    def _():
        tiles = lax.broadcasted_iota(jnp.int32, (1, TD * G), 1) // G
        first = jnp.zeros((1, TD * G), jnp.int32)
        second, seed = first, first
        for t in range(TD):
            first = jnp.where(tiles == t, pairs[2 * t], first)
            second = jnp.where(tiles == t, pairs[2 * t + 1], second)
            seed = jnp.where(tiles == t, seeds[t], seed)
        flip = 1 - 2 * (seed >> 29 & 1)
        row = lax.broadcasted_iota(jnp.int32, (G, TD * G), 0)
        meta[...] = jnp.where(row == 0, first, jnp.where(row == 1, second, flip)).astype(F32)


def mix(which, seeds, pairs, matrix, mixers):
    width = matrix.shape[1]
    return pl.pallas_call(
        mix_kernel,
        out_shape=(
            jax.ShapeDtypeStruct((TILE // G, TD * G, width), BF16),
            jax.ShapeDtypeStruct((G, TD * G), F32),
        ),
        grid_spec=pltpu.PrefetchScalarGridSpec(
            num_scalar_prefetch=3,
            grid=(TD // STEP_TILES,),
            in_specs=[
                pl.BlockSpec((STEP_TILES * TILE, width), lambda i, a, b, c: (i, 0)),
                pl.BlockSpec(mixers.shape, lambda i, a, b, c: (0, 0, 0)),
            ],
            out_specs=(
                pl.BlockSpec((TILE // G, STEP_TILES * G, width), lambda i, a, b, c: (0, i, 0)),
                pl.BlockSpec((G, TD * G), lambda i, a, b, c: (0, 0)),
            ),
        ),
        name="mix",
    )(which, seeds, pairs, matrix, mixers)


def selection(meta):
    row = lax.broadcasted_iota(jnp.int32, (NB * G, TD * G), 0)
    lane = lax.broadcasted_iota(jnp.int32, (NB * G, TD * G), 1)
    first = meta[0:1, :].astype(jnp.int32)
    second = meta[1:2, :].astype(jnp.int32)
    flip = meta[2:3, :]
    bucket = row >> 3
    value = jnp.where(bucket == first, 1.0, 0.0) + jnp.where(bucket == second, flip, 0.0)
    return jnp.where((row & 7) == (lane & 7), value, 0.0).astype(BF16)


def scatter_kernel(m_ref, sel_ref, x_ref, other_ref, send, recv, local, sel_sems):
    z, k, x, y = place()
    col = x * NX + y
    source = col == 0
    sibling = {"k": 1 - k}
    hello(sibling)
    for ks in range(NK):
        @pl.when(jnp.logical_not(source))
        def _():
            hello({"k": ks, "x": 0, "y": 0})

    @pl.when(source)
    def _():
        meet(NK * NC - 1)

    @pl.when(jnp.logical_not(source))
    def _():
        meet(1)

    swap = remote(sel_ref, other_ref, sel_sems.at[0], sel_sems.at[1], sibling)
    swap.start()

    def piece(c, kd):
        part = m_ref.at[c, :, pl.ds(pl.multiple_of(kd * HALF, HALF), HALF)]
        return remote(
            part, x_ref.at[k], send.at[c, kd], recv.at[k], {"k": kd, "x": c // NX, "y": c % NX}
        )

    own = pltpu.make_async_copy(
        m_ref.at[0, :, pl.ds(pl.multiple_of(k * HALF, HALF), HALF)], x_ref.at[k], local
    )

    @pl.when(source)
    def _():
        for c in range(1, NC):
            for kd in range(NK):
                piece(c, kd).start()
        piece(0, 1 - k).start()
        own.start()
        own.wait()
        for c in range(1, NC):
            for kd in range(NK):
                piece(c, kd).wait_send()
        piece(0, 1 - k).wait_send()
        remote(x_ref.at[1 - k], x_ref.at[1 - k], send.at[0, 0], recv.at[1 - k], sibling).wait_recv()

    @pl.when(jnp.logical_not(source))
    def _():
        for ks in range(NK):
            remote(x_ref.at[ks], x_ref.at[ks], send.at[0, 0], recv.at[ks], sibling).wait_recv()

    swap.wait()


ANY = pl.BlockSpec(memory_space=pl.ANY)
VM = pl.BlockSpec(memory_space=pltpu.VMEM)
DMA = pltpu.SemaphoreType.DMA


def scatter(mixed, sel):
    return pl.pallas_call(
        scatter_kernel,
        out_shape=(
            jax.ShapeDtypeStruct((NK, TD * G, HALF), BF16),
            jax.ShapeDtypeStruct(sel.shape, F32),
        ),
        in_specs=[ANY, ANY],
        out_specs=(ANY, ANY),
        scratch_shapes=[DMA((NC, NK)), DMA((NK,)), DMA, DMA((2,))],
        compiler_params=pltpu.CompilerParams(collective_id=1, has_side_effects=True),
        name="scatter",
    )(mixed, sel)


def total_kernel(x_ref, mine_ref, other_ref, p_ref, y_ref, got, send_a, recv_a, send_b, recv_b, send_c, recv_c):
    z, k, x, y = place()
    sibling = {"k": 1 - k}
    hello(sibling)
    for d in range(1, NZ):
        hello({"z": lax.rem(z + d, NZ)})
    part = jnp.dot(selection(mine_ref[...]), x_ref[k], preferred_element_type=F32)
    part = part + jnp.dot(selection(other_ref[...]), x_ref[1 - k], preferred_element_type=F32)
    y_ref[...] = part.reshape(y_ref.shape)
    meet(NZ)
    for d in range(1, NZ):
        zt = lax.rem(z + d, NZ)
        remote(y_ref.at[zt], got.at[d - 1], send_a.at[d - 1], recv_a.at[d - 1], {"z": zt}).start()
    acc = y_ref[z]
    for d in range(1, NZ):
        remote(got.at[d - 1], got.at[d - 1], send_a.at[d - 1], recv_a.at[d - 1], sibling).wait_recv()
        acc = acc + got[d - 1]
    p_ref[k, z] = acc
    for d in range(1, NZ):
        zt = lax.rem(z + d, NZ)
        remote(p_ref.at[k, z], p_ref.at[k, z], send_b.at[d - 1], recv_b.at[d - 1], {"z": zt}).start()

    def hand(d):
        zs = lax.rem(z + NZ - d, NZ)
        return remote(p_ref.at[k, zs], p_ref.at[k, zs], send_c.at[d], recv_c.at[d], sibling)

    hand(0).start()
    for d in range(1, NZ):
        zs = lax.rem(z + NZ - d, NZ)
        remote(p_ref.at[k, zs], p_ref.at[k, zs], send_b.at[d - 1], recv_b.at[d - 1], sibling).wait_recv()
        hand(d).start()
    for d in range(NZ):
        zs = lax.rem(z + NZ - d, NZ)
        remote(
            p_ref.at[1 - k, zs], p_ref.at[1 - k, zs], send_c.at[d], recv_c.at[d], sibling
        ).wait_recv()
    for d in range(1, NZ):
        remote(got.at[d - 1], got.at[d - 1], send_a.at[d - 1], recv_a.at[d - 1], sibling).wait_send()
        remote(p_ref.at[k, z], p_ref.at[k, z], send_b.at[d - 1], recv_b.at[d - 1], sibling).wait_send()
    for d in range(NZ):
        hand(d).wait_send()


def total(panel, mine, other):
    rows = NB * G // NZ
    return pl.pallas_call(
        total_kernel,
        out_shape=jax.ShapeDtypeStruct((NK, NZ, rows, HALF), F32),
        in_specs=[VM, VM, VM],
        out_specs=VM,
        scratch_shapes=[
            pltpu.VMEM((NZ, rows, HALF), F32),
            pltpu.VMEM((NZ - 1, rows, HALF), F32),
            DMA((NZ - 1,)),
            DMA((NZ - 1,)),
            DMA((NZ - 1,)),
            DMA((NZ - 1,)),
            DMA((NZ,)),
            DMA((NZ,)),
        ],
        compiler_params=pltpu.CompilerParams(collective_id=2, has_side_effects=True),
        name="total",
    )(panel, mine, other)


def share_kernel(p_ref, meta_ref, all_ref, gram_ref, w_ref, g_ref, got, send_w, recv_w, send_g, recv_g, send_h, recv_h, local):
    z, k, x, y = place()
    col = x * NX + y

    def plane(d):
        other = lax.rem(k * NC + col + d, NK * NC)
        c = lax.rem(other, NC)
        return other // NC, c, {"k": other // NC, "x": c // NX, "y": lax.rem(c, NX)}

    for d in range(1, NK * NC):
        hello(plane(d)[2])
    sketch = jnp.concatenate([p_ref[0].reshape(NB * G, HALF), p_ref[1].reshape(NB * G, HALF)], axis=1)
    turned = sketch.T
    g_ref[...] = dot(turned, sketch)
    w_ref[...] = dot(turned, selection(meta_ref[...]).astype(F32))
    meet(NK * NC - 1)

    def rows_of(kk, c):
        return pl.ds(pl.multiple_of(kk * HALF + c * G, G), G)

    quarter = PS // 4

    def slot(h, c, s):
        return all_ref.at[c, pl.ds((2 * h + s) * quarter, quarter), :]

    def to(h, stage, direction):
        along_x = (h == 0) == (stage == 0)
        step = 1 if direction == 0 else NX - 1
        if along_x:
            return {"x": lax.rem(x + step, NX)}
        return {"y": lax.rem(y + step, NX)}

    def index(h, a, b):
        if h == 0:
            return lax.rem(x + a, NX) * NX + lax.rem(y + b, NX)
        return lax.rem(x + b, NX) * NX + lax.rem(y + a, NX)

    def move(h, a, b, s, stage, direction, first=None):
        c = index(h, a, b)
        src = slot(h, c, s) if first is None else first
        return remote(src, slot(h, c, s), send_w.at[h, c, s, stage, direction], recv_w.at[h, c, s], to(h, stage, direction))

    def arrived(h, a, b, s):
        c = index(h, a, b)
        remote(
            slot(h, c, s), slot(h, c, s), send_w.at[h, c, s, 0, 0], recv_w.at[h, c, s], {"k": 1 - k}
        ).wait_recv()

    sent = []

    def go(copy):
        copy.start()
        sent.append(copy)

    for d in range(1, NC):
        c = lax.rem(col + d, NC)
        go(
            remote(
                g_ref.at[rows_of(k, c), :],
                got.at[d - 1],
                send_g.at[d - 1],
                recv_g.at[d - 1],
                {"x": c // NX, "y": lax.rem(c, NX)},
            )
        )
    keep = pltpu.make_async_copy(w_ref, all_ref.at[col], local)
    keep.start()

    own = lambda h, s: w_ref.at[pl.ds((2 * h + s) * quarter, quarter), :]
    for s in range(2):
        for h in range(2):
            go(move(h, 0, 0, s, 0, s, own(h, s)))
    for s in range(2):
        for h in range(2):
            go(move(h, 0, 0, s, 0, 1 - s, own(h, s)))
    for s in range(2):
        for h in range(2):
            go(move(h, 0, 0, s, 1, s, own(h, s)))
    for s in range(2):
        for h in range(2):
            go(move(h, 0, 0, s, 1, 1 - s, own(h, s)))
    for h in range(2):
        arrived(h, 3, 0, 0)
        go(move(h, 3, 0, 0, 0, 0))
        arrived(h, 1, 0, 1)
        go(move(h, 1, 0, 1, 0, 1))
    for h in range(2):
        for a, s in ((3, 0), (1, 1)):
            go(move(h, a, 0, s, 1, s))
            go(move(h, a, 0, s, 1, 1 - s))
    for h in range(2):
        for a, s in ((3, 1), (1, 0)):
            arrived(h, a, 0, s)
            go(move(h, a, 0, s, 1, s))
            go(move(h, a, 0, s, 1, 1 - s))

    acc = g_ref[rows_of(k, col), :]
    for d in range(1, NC):
        remote(got.at[d - 1], got.at[d - 1], send_g.at[d - 1], recv_g.at[d - 1], {"k": 1 - k}).wait_recv()
        acc = acc + got[d - 1]
    gram_ref[rows_of(k, col), :] = acc
    mine = gram_ref.at[rows_of(k, col), :]
    for d in range(1, NK * NC):
        go(remote(mine, mine, send_h.at[d - 1], recv_h.at[d - 1], plane(d)[2]))

    for h in range(2):
        for s in range(2):
            arrived(h, 2, 0, s)
            go(move(h, 2, 0, s, 1, s))
            go(move(h, 2, 0, s, 1, 1 - s))
    for a in (0, 3, 1, 2):
        for h in range(2):
            arrived(h, a, 3, 0)
            go(move(h, a, 3, 0, 1, 0))
            arrived(h, a, 1, 1)
            go(move(h, a, 1, 1, 1, 1))
    for h in range(2):
        for a in (0, 3, 1, 2):
            arrived(h, a, 3, 1)
            arrived(h, a, 1, 0)
            for s in range(2):
                arrived(h, a, 2, s)
    for d in range(1, NK * NC):
        kk, c, where = plane(NK * NC - d)
        theirs = gram_ref.at[rows_of(kk, c), :]
        remote(theirs, theirs, send_h.at[d - 1], recv_h.at[d - 1], {"k": 1 - k}).wait_recv()
    for copy in sent:
        copy.wait_send()
    keep.wait()


def share(sketch, meta):
    return pl.pallas_call(
        share_kernel,
        out_shape=(
            jax.ShapeDtypeStruct((NC, PS, TD * G), F32),
            jax.ShapeDtypeStruct((PS, PS), F32),
        ),
        in_specs=[VM, VM],
        out_specs=(VM, VM),
        scratch_shapes=[
            pltpu.VMEM((PS, TD * G), F32),
            pltpu.VMEM((PS, PS), F32),
            pltpu.VMEM((NC - 1, G, PS), F32),
            DMA((2, NC, 2, 2, 2)),
            DMA((2, NC, 2)),
            DMA((NC - 1,)),
            DMA((NC - 1,)),
            DMA((NK * NC - 1,)),
            DMA((NK * NC - 1,)),
            DMA,
        ],
        compiler_params=pltpu.CompilerParams(collective_id=3, has_side_effects=True),
        name="share",
    )(sketch, meta)


NBK = 64


def invert_block(block):
    n = NBK
    ident = (lax.broadcasted_iota(jnp.int32, (n, n), 0) == lax.broadcasted_iota(jnp.int32, (n, n), 1)).astype(F32)
    aug = jnp.concatenate([block, ident], axis=1)
    groups = n // G
    rows = [aug[g * G : (g + 1) * G, :] for g in range(groups)]
    sub = lax.broadcasted_iota(jnp.int32, (G, 2 * n), 0)
    for g in range(groups):
        cols = [
            {h: jnp.broadcast_to(rows[h][:, g * G + i : g * G + i + 1], (G, 2 * n)) for h in range(g, groups)}
            for i in range(G)
        ]
        scale = jnp.zeros((G, 2 * n), F32)
        for i in range(G):
            pivot = jnp.broadcast_to(cols[i][g][i : i + 1, :], (G, 2 * n))
            inv = 1.0 / pivot
            scale = jnp.where(sub == i, lax.rsqrt(pivot), scale)
            below = dict(cols[i])
            below[g] = jnp.where(sub > i, below[g], 0.0)
            for m in range(i + 1, G):
                f = jnp.broadcast_to(cols[m][g][i : i + 1, :], (G, 2 * n)) * inv
                for h in range(g, groups):
                    cols[m][h] = cols[m][h] - below[h] * f
            u = jnp.broadcast_to(rows[g][i : i + 1, :], (G, 2 * n)) * inv
            for h in range(g, groups):
                rows[h] = rows[h] - below[h] * u
        rows[g] = rows[g] * scale
    done = jnp.concatenate(rows, axis=0)
    return done[:, n:]


def inverse_factor(gram_ref, work):
    n = PS
    work[:, :n] = gram_ref[...]
    work[:, n:] = (lax.broadcasted_iota(jnp.int32, (n, n), 0) == lax.broadcasted_iota(jnp.int32, (n, n), 1)).astype(F32)
    for p in range(n // NBK):
        lo, hi = p * NBK, (p + 1) * NBK
        inv = invert_block(work[lo:hi, lo:hi])
        row = dot(inv, work[lo:hi, :])
        work[lo:hi, :] = row
        if hi < n:
            work[hi:, :] = work[hi:, :] - dot(row[:, hi:n].T, row)


def factor_kernel(gram_ref, out, work):
    inverse_factor(gram_ref, work)
    out[...] = work[:, PS:]


def factor(gram):
    return pl.pallas_call(
        factor_kernel,
        out_shape=jax.ShapeDtypeStruct((PS, PS), F32),
        in_specs=[VM],
        out_specs=VM,
        scratch_shapes=[pltpu.VMEM((PS, 2 * PS), F32)],
        name="factor",
    )(gram)


def finish_kernel(w_ref, m_ref, inv_ref, o_ref, value, summed, pair, got, send, recv, pair_sems):
    z, k, x, y = place()
    sibling = {"k": 1 - k}
    hello(sibling)
    for d in range(1, NZ):
        hello({"z": lax.rem(z + d, NZ)})

    def add(c, acc):
        w = w_ref[c]
        high = w.astype(BF16)
        rest = w - high.astype(F32)
        low = rest.astype(BF16)
        last = (rest - low.astype(F32)).astype(BF16)
        m = m_ref[c]
        for part in (high, low, last):
            acc = acc + jnp.dot(part, m, preferred_element_type=F32)
        return acc

    cross = lax.fori_loop(0, NC, add, jnp.zeros((PS, m_ref.shape[2]), F32))
    value[...] = dot(inv_ref[...], cross).reshape(value.shape)
    meet(NZ)
    swap = remote(value.at[:, 1 - k], pair, pair_sems.at[0], pair_sems.at[1], sibling)
    swap.start()
    swap.wait_recv()
    summed[...] = value[:, k] + pair[...]

    def copy(d):
        zt = lax.rem(z + d, NZ)
        return remote(summed.at[zt], got.at[d - 1], send.at[d - 1], recv.at[d - 1], {"z": zt})

    for d in range(1, NZ):
        copy(d).start()
    acc = summed[z]
    for d in range(1, NZ):
        copy(d).wait_recv()
        acc = acc + got[d - 1]
    o_ref[...] = acc
    for d in range(1, NZ):
        copy(d).wait_send()
    swap.wait_send()


def finish(weights, mixed, inverse):
    width = mixed.shape[2]
    return pl.pallas_call(
        finish_kernel,
        out_shape=jax.ShapeDtypeStruct((G, width), F32),
        in_specs=[VM, VM, VM],
        out_specs=VM,
        scratch_shapes=[
            pltpu.VMEM((NZ, NK, G, width), F32),
            pltpu.VMEM((NZ, G, width), F32),
            pltpu.VMEM((NZ, G, width), F32),
            pltpu.VMEM((NZ - 1, G, width), F32),
            DMA((NZ - 1,)),
            DMA((NZ - 1,)),
            DMA((2,)),
        ],
        compiler_params=pltpu.CompilerParams(collective_id=4, has_side_effects=True),
        name="finish",
    )(weights, mixed, inverse)


def local(matrix, mixers, bucket_pair, mixer_index, sign_seed):
    mixed, meta = mix(mixer_index, sign_seed, bucket_pair.reshape(-1), matrix, mixers)
    panel, other = scatter(mixed, meta)
    sketch = total(panel, meta, other)
    weights, gram = share(sketch, meta)
    return finish(weights, mixed, factor(gram))


def solution(mesh):
    split = Mesh(mesh.devices.reshape(NZ, NK, NX, NX), ("z", "k", "x", "y"))
    return jax.shard_map(
        local,
        mesh=split,
        in_specs=(P(ROWS, COLS), P(), P(ROWS, None), P(ROWS), P(ROWS)),
        out_specs=P(ROWS, COLS),
        check_vma=False,
    )
```

```python
import functools

import jax
import jax.numpy as jnp
from jax import lax
from jax.experimental import pallas as pl
from jax.experimental.pallas import tpu as pltpu
from jax.sharding import Mesh
from jax.sharding import PartitionSpec as P

TILE = 128
PS = 256
NB = 64
TD = 32
NZ = 16
NK = 2
NX = 4
NC = 16
G = 8
HALF = 128
MESH = pl.DeviceIdType.MESH
HI = lax.Precision.HIGHEST
ROWS = ("z", "k")
COLS = ("x", "y")
F32 = jnp.float32
BF16 = jnp.bfloat16


def place():
    return tuple(lax.axis_index(a) for a in ("z", "k", "x", "y"))


def remote(src, dst, send, recv, to):
    return pltpu.make_async_remote_copy(
        src_ref=src, dst_ref=dst, send_sem=send, recv_sem=recv, device_id=to, device_id_type=MESH
    )


def hello(to):
    pl.semaphore_signal(pltpu.get_barrier_semaphore(), inc=1, device_id=to, device_id_type=MESH)


def meet(count):
    pl.semaphore_wait(pltpu.get_barrier_semaphore(), count)


def dot(a, b):
    return jnp.dot(a, b, precision=HI, preferred_element_type=F32)


def selection(meta):
    row = lax.broadcasted_iota(jnp.int32, (NB * G, TD * G), 0)
    lane = lax.broadcasted_iota(jnp.int32, (NB * G, TD * G), 1)
    first = meta[0:1, :].astype(jnp.int32)
    second = meta[1:2, :].astype(jnp.int32)
    flip = meta[2:3, :]
    bucket = row >> 3
    value = jnp.where(bucket == first, 1.0, 0.0) + jnp.where(bucket == second, flip, 0.0)
    return jnp.where((row & 7) == (lane & 7), value, 0.0).astype(BF16)


NBK = 64


def invert_block(block):
    n = NBK
    ident = (lax.broadcasted_iota(jnp.int32, (n, n), 0) == lax.broadcasted_iota(jnp.int32, (n, n), 1)).astype(F32)
    aug = jnp.concatenate([block, ident], axis=1)
    groups = n // G
    rows = [aug[g * G : (g + 1) * G, :] for g in range(groups)]
    sub = lax.broadcasted_iota(jnp.int32, (G, 2 * n), 0)
    for g in range(groups):
        cols = [
            {h: jnp.broadcast_to(rows[h][:, g * G + i : g * G + i + 1], (G, 2 * n)) for h in range(g, groups)}
            for i in range(G)
        ]
        scale = jnp.zeros((G, 2 * n), F32)
        for i in range(G):
            pivot = jnp.broadcast_to(cols[i][g][i : i + 1, :], (G, 2 * n))
            inv = 1.0 / pivot
            scale = jnp.where(sub == i, lax.rsqrt(pivot), scale)
            below = dict(cols[i])
            below[g] = jnp.where(sub > i, below[g], 0.0)
            for m in range(i + 1, G):
                f = jnp.broadcast_to(cols[m][g][i : i + 1, :], (G, 2 * n)) * inv
                for h in range(g, groups):
                    cols[m][h] = cols[m][h] - below[h] * f
            u = jnp.broadcast_to(rows[g][i : i + 1, :], (G, 2 * n)) * inv
            for h in range(g, groups):
                rows[h] = rows[h] - below[h] * u
        rows[g] = rows[g] * scale
    done = jnp.concatenate(rows, axis=0)
    return done[:, n:]


def start_factor(gram, work):
    work[:, :PS] = gram
    work[:, PS:] = (
        lax.broadcasted_iota(jnp.int32, (PS, PS), 0) == lax.broadcasted_iota(jnp.int32, (PS, PS), 1)
    ).astype(F32)


def factor_step(work, p):
    lo, hi = p * NBK, (p + 1) * NBK
    inv = invert_block(work[lo:hi, lo:hi])
    row = dot(inv, work[lo:hi, :])
    work[lo:hi, :] = row
    if hi < PS:
        work[hi:, :] = work[hi:, :] - dot(row[:, hi:PS].T, row)


VM = pl.BlockSpec(memory_space=pltpu.VMEM)
SM = pl.BlockSpec(memory_space=pltpu.SMEM)
DMA = pltpu.SemaphoreType.DMA
STEP_TILES = 8
QUARTER = PS // 4
OWN_ROWS = NB * G // NZ
RELAYS = ((4, (8, 5, 7)), (12, (14, 13, 15)), (1, (10, 9, 2)), (3, (6, 11)))


def mix_tiles(which, seeds, pairs, mat, mixers, m_ref, meta_ref):
    lane = lax.broadcasted_iota(jnp.int32, (1, TILE), 1) * 40503

    def some(step, carry):
        for pair in range(STEP_TILES // 2):
            parts = []
            for q in range(2):
                tile = step * STEP_TILES + 2 * pair + q
                hashed = (seeds[tile] ^ lane) * 69069
                sign = (1 - 2 * ((hashed >> 16) & 1)).astype(F32)
                mixer = mixers[which[tile]] * sign
                block = mat[pl.ds(pl.multiple_of(tile * TILE, TILE), TILE), :]
                parts.append(dot(mixer, block).reshape(TILE // G, G, mat.shape[1]))
            at = pl.multiple_of((step * STEP_TILES + 2 * pair) * G, 2 * G)
            m_ref[:, pl.ds(at, 2 * G), :] = jnp.concatenate(parts, axis=1).astype(BF16)
        return carry

    lax.fori_loop(0, TD // STEP_TILES, some, 0)
    tiles = lax.broadcasted_iota(jnp.int32, (1, TD * G), 1) // G
    first = jnp.zeros((1, TD * G), jnp.int32)
    second, seed = first, first
    for t in range(TD):
        first = jnp.where(tiles == t, pairs[t, 0], first)
        second = jnp.where(tiles == t, pairs[t, 1], second)
        seed = jnp.where(tiles == t, seeds[t], seed)
    flip = 1 - 2 * (seed >> 29 & 1)
    row = lax.broadcasted_iota(jnp.int32, (G, TD * G), 0)
    meta_ref[...] = jnp.where(row == 0, first, jnp.where(row == 1, second, flip)).astype(F32)


def main_kernel(
    which, seeds, pairs, mat, mixers, o_ref,
    m_ref, meta_ref, other_ref, x_ref, relay, y_ref, got_y, p_ref,
    w_ref, all_ref, g_ref, got_g, gram_ref, work, value, summed, pair, got_v,
    meta_sems, send_x, recv_x, send_r, recv_r,
    send_a, recv_a, send_b, recv_b, send_c, recv_c,
    send_w, recv_w, send_g, recv_g, send_h, recv_h,
    pair_sems, send_v, recv_v,
):
    z, k, x, y = place()
    col = x * NX + y
    source = col == 0
    sibling = {"k": 1 - k}

    def plane(d):
        other = lax.rem(k * NC + col + d, NK * NC)
        c = lax.rem(other, NC)
        return other // NC, c, {"k": other // NC, "x": c // NX, "y": lax.rem(c, NX)}

    def up(d):
        return lax.rem(z + d, NZ)

    for d in range(1, NK * NC):
        hello(plane(d)[2])
    for d in range(1, NZ):
        hello({"z": up(d)})
    mix_tiles(which, seeds, pairs, mat, mixers, m_ref, meta_ref)
    meet(NK * NC - 1 + NZ - 1)

    sent = []

    def go(copy):
        copy.start()
        sent.append(copy)

    def landed(ref, recv):
        remote(ref, ref, send_x.at[0, 0], recv, sibling).wait_recv()

    def half(c, kd):
        return m_ref.at[c, :, kd * HALF : (kd + 1) * HALF]

    def spot(c):
        return {"x": c // NX, "y": c % NX}

    pieces = []
    for j in range(3):
        for first, rest in RELAYS:
            if j < len(rest):
                for kd in range(NK):
                    c = rest[j]
                    pieces.append((half(c, kd), relay.at[j, kd], send_x.at[c, kd], recv_r.at[j, kd], spot(first)))
    for first, rest in RELAYS:
        for kd in range(NK):
            pieces.append(
                (half(first, kd), x_ref.at[k], send_x.at[first, kd], recv_x.at[k], {"k": kd, **spot(first)})
            )
    cross_half = m_ref.at[0, :, pl.ds(pl.multiple_of((1 - k) * HALF, HALF), HALF)]
    pieces.append((cross_half, x_ref.at[k], send_x.at[0, 0], recv_x.at[k], sibling))

    @pl.when(source)
    def _():
        for piece in pieces:
            remote(*piece).start()
        x_ref[k] = jnp.where(k == 0, m_ref[0, :, :HALF], m_ref[0, :, HALF:])

    go(remote(meta_ref, other_ref, meta_sems.at[0], meta_sems.at[1], sibling))

    def onward(j, kd, c):
        return remote(relay.at[j, kd], x_ref.at[k], send_r.at[j, kd], recv_x.at[k], {"k": kd, **spot(c)})

    for first, rest in RELAYS:
        @pl.when(col == first)
        def _():
            for j, c in enumerate(rest):
                for kd in range(NK):
                    landed(relay.at[j, kd], recv_r.at[j, kd])
                    onward(j, kd, c).start()

    landed(other_ref, meta_sems.at[1])
    mine = selection(meta_ref[...])
    theirs = selection(other_ref[...])

    @pl.when(jnp.logical_not(source))
    def _():
        landed(x_ref.at[k], recv_x.at[k])

    landed(x_ref.at[1 - k], recv_x.at[1 - k])
    part = jnp.dot(mine, x_ref[k], preferred_element_type=F32)
    part = part + jnp.dot(theirs, x_ref[1 - k], preferred_element_type=F32)
    y_ref[...] = part.reshape(y_ref.shape)

    for d in range(1, NZ):
        go(remote(y_ref.at[up(d)], got_y.at[d - 1], send_a.at[d - 1], recv_a.at[d - 1], {"z": up(d)}))
    acc = y_ref[z]
    for d in range(1, NZ):
        landed(got_y.at[d - 1], recv_a.at[d - 1])
        acc = acc + got_y[d - 1]
    p_ref[k, z] = acc
    for d in range(1, NZ):
        go(remote(p_ref.at[k, z], p_ref.at[k, z], send_b.at[d - 1], recv_b.at[d - 1], {"z": up(d)}))
    go(remote(p_ref.at[k, z], p_ref.at[k, z], send_c.at[0], recv_c.at[0], sibling))
    for d in range(1, NZ):
        zs = up(NZ - d)
        landed(p_ref.at[k, zs], recv_b.at[d - 1])
        go(remote(p_ref.at[k, zs], p_ref.at[k, zs], send_c.at[d], recv_c.at[d], sibling))
    for d in range(NZ):
        landed(p_ref.at[1 - k, up(NZ - d)], recv_c.at[d])

    sketch = jnp.concatenate([p_ref[0].reshape(NB * G, HALF), p_ref[1].reshape(NB * G, HALF)], axis=1)
    turned = sketch.T
    g_ref[...] = dot(turned, sketch)
    w_ref[...] = dot(turned, selection(meta_ref[...]).astype(F32))

    def rows_of(kk, c):
        return pl.ds(pl.multiple_of(kk * HALF + c * G, G), G)

    for d in range(1, NC):
        c = lax.rem(col + d, NC)
        go(
            remote(
                g_ref.at[rows_of(k, c), :], got_g.at[d - 1], send_g.at[d - 1], recv_g.at[d - 1],
                {"x": c // NX, "y": lax.rem(c, NX)},
            )
        )

    def piece_of(h, s):
        return pl.ds((2 * h + s) * QUARTER, QUARTER)

    def index(h, a, b):
        if h == 0:
            return lax.rem(x + a, NX) * NX + lax.rem(y + b, NX)
        return lax.rem(x + b, NX) * NX + lax.rem(y + a, NX)

    def send(h, a, b, s, stage, direction):
        c = index(h, a, b)
        there = all_ref.at[c, piece_of(h, s), :]
        here = w_ref.at[piece_of(h, s), :] if a == b == 0 else there
        step = 1 if direction == 0 else NX - 1
        to = {"x": lax.rem(x + step, NX)} if (h == 0) == (stage == 0) else {"y": lax.rem(y + step, NX)}
        go(remote(here, there, send_w.at[h, c, s, stage, direction], recv_w.at[h, c, s], to))

    seen = {(h, 0, 0, s) for h in range(2) for s in range(2)}

    def arrived(h, a, b, s):
        if (h, a, b, s) not in seen:
            seen.add((h, a, b, s))
            c = index(h, a, b)
            landed(all_ref.at[c, piece_of(h, s), :], recv_w.at[h, c, s])

    def across(h, a, s):
        arrived(h, a, 0, s)
        send(h, a, 0, s, 1, s)
        send(h, a, 0, s, 1, 1 - s)

    def pass_on(a):
        for h in range(2):
            arrived(h, a, 3, 0)
            send(h, a, 3, 0, 1, 0)
            arrived(h, a, 1, 1)
            send(h, a, 1, 1, 1, 1)

    for stage in range(2):
        for turn in range(2):
            for s in range(2):
                for h in range(2):
                    send(h, 0, 0, s, stage, s if turn == 0 else 1 - s)

    acc = g_ref[rows_of(k, col), :]
    for d in range(1, NC):
        landed(got_g.at[d - 1], recv_g.at[d - 1])
        acc = acc + got_g[d - 1]
    gram_ref[rows_of(k, col), :] = acc
    for d in range(1, NK * NC):
        own = gram_ref.at[rows_of(k, col), :]
        go(remote(own, own, send_h.at[d - 1], recv_h.at[d - 1], plane(d)[2]))

    for h in range(2):
        arrived(h, 3, 0, 0)
        send(h, 3, 0, 0, 0, 0)
        arrived(h, 1, 0, 1)
        send(h, 1, 0, 1, 0, 1)
    for a, s in ((3, 0), (1, 1), (3, 1), (1, 0)):
        for h in range(2):
            across(h, a, s)
    for d in range(1, NK * NC):
        kk, c, _ = plane(NK * NC - d)
        landed(gram_ref.at[rows_of(kk, c), :], recv_h.at[d - 1])
    all_ref[col] = w_ref[...]
    start_factor(gram_ref[...], work)
    factor_step(work, 0)
    for h in range(2):
        for s in range(2):
            across(h, 2, s)
    pass_on(0)
    factor_step(work, 1)
    pass_on(3)
    pass_on(1)
    factor_step(work, 2)
    pass_on(2)
    factor_step(work, 3)

    def ready(dx, dy):
        for s in range(2):
            arrived(0, dx, dy, s)
            arrived(1, dy, dx, s)

    def add(dx, dy, acc):
        c = lax.rem(x + dx, NX) * NX + lax.rem(y + dy, NX)
        w = all_ref[c]
        high = w.astype(BF16)
        rest = w - high.astype(F32)
        low = rest.astype(BF16)
        last = (rest - low.astype(F32)).astype(BF16)
        tiles = m_ref[c]
        for part in (high, low, last):
            acc = acc + jnp.dot(part, tiles, preferred_element_type=F32)
        return acc

    cross = jnp.zeros((PS, m_ref.shape[2]), F32)
    for d in range(NX):
        ready(d, 0)
        ready(0, d)
    cross = lax.fori_loop(
        0, 2 * NX - 1, lambda j, acc: add(jnp.where(j < NX, j, 0), jnp.where(j < NX, 0, j - NX + 1), acc), cross
    )
    for dx in range(1, NX):
        for dy in range(1, NX):
            ready(dx, dy)
    cross = lax.fori_loop(0, (NX - 1) ** 2, lambda j, acc: add(1 + j // 3, 1 + lax.rem(j, 3), acc), cross)
    value[...] = dot(work[:, PS:], cross).reshape(value.shape)
    go(remote(value.at[:, 1 - k], pair, pair_sems.at[0], pair_sems.at[1], sibling))
    landed(pair, pair_sems.at[1])
    summed[...] = value[:, k] + pair[...]
    for d in range(1, NZ):
        go(remote(summed.at[up(d)], got_v.at[d - 1], send_v.at[d - 1], recv_v.at[d - 1], {"z": up(d)}))
    acc = summed[z]
    for d in range(1, NZ):
        landed(got_v.at[d - 1], recv_v.at[d - 1])
        acc = acc + got_v[d - 1]
    o_ref[...] = acc

    @pl.when(source)
    def _():
        for piece in pieces:
            remote(*piece).wait_send()

    for first, rest in RELAYS:
        @pl.when(col == first)
        def _():
            for j, c in enumerate(rest):
                for kd in range(NK):
                    onward(j, kd, c).wait_send()

    for copy in sent:
        copy.wait_send()


def local(matrix, mixers, bucket_pair, mixer_index, sign_seed):
    width = matrix.shape[1]
    one, two, plane = (NZ - 1,), (2,), (NK * NC - 1,)
    return pl.pallas_call(
        main_kernel,
        out_shape=jax.ShapeDtypeStruct((G, width), F32),
        in_specs=[SM, SM, SM, VM, VM],
        out_specs=VM,
        scratch_shapes=[
            pltpu.VMEM((NC, TD * G, width), BF16),
            pltpu.VMEM((G, TD * G), F32),
            pltpu.VMEM((G, TD * G), F32),
            pltpu.VMEM((NK, TD * G, HALF), BF16),
            pltpu.VMEM((3, NK, TD * G, HALF), BF16),
            pltpu.VMEM((NZ, OWN_ROWS, HALF), F32),
            pltpu.VMEM((NZ - 1, OWN_ROWS, HALF), F32),
            pltpu.VMEM((NK, NZ, OWN_ROWS, HALF), F32),
            pltpu.VMEM((PS, TD * G), F32),
            pltpu.VMEM((NC, PS, TD * G), F32),
            pltpu.VMEM((PS, PS), F32),
            pltpu.VMEM((NC - 1, G, PS), F32),
            pltpu.VMEM((PS, PS), F32),
            pltpu.VMEM((PS, 2 * PS), F32),
            pltpu.VMEM((NZ, NK, G, width), F32),
            pltpu.VMEM((NZ, G, width), F32),
            pltpu.VMEM((NZ, G, width), F32),
            pltpu.VMEM((NZ - 1, G, width), F32),
            DMA(two), DMA((NC, NK)), DMA(two), DMA((3, NK)), DMA((3, NK)),
            DMA(one), DMA(one), DMA(one), DMA(one), DMA((NZ,)), DMA((NZ,)),
            DMA((2, NC, 2, 2, 2)), DMA((2, NC, 2)), DMA((NC - 1,)), DMA((NC - 1,)), DMA(plane), DMA(plane),
            DMA(two), DMA(one), DMA(one),
        ],
        compiler_params=pltpu.CompilerParams(collective_id=1, has_side_effects=True),
        name="main",
    )(mixer_index, sign_seed, bucket_pair, matrix, mixers)


def solution(mesh):
    split = Mesh(mesh.devices.reshape(NZ, NK, NX, NX), ("z", "k", "x", "y"))
    return jax.shard_map(
        local,
        mesh=split,
        in_specs=(P(ROWS, COLS), P(), P(ROWS, None), P(ROWS), P(ROWS)),
        out_specs=P(ROWS, COLS),
        check_vma=False,
    )
```

```python
import functools

import jax
import jax.numpy as jnp
from jax import lax
from jax.experimental import pallas as pl
from jax.experimental.pallas import tpu as pltpu
from jax.sharding import Mesh
from jax.sharding import PartitionSpec as P

TILE = 128
PS = 256
NB = 64
TD = 32
NZ = 16
NK = 2
NX = 4
NC = 16
G = 8
HALF = 128
MESH = pl.DeviceIdType.MESH
HI = lax.Precision.HIGHEST
ROWS = ("z", "k")
COLS = ("x", "y")
F32 = jnp.float32
BF16 = jnp.bfloat16


def place():
    return tuple(lax.axis_index(a) for a in ("z", "k", "x", "y"))


def remote(src, dst, send, recv, to):
    return pltpu.make_async_remote_copy(
        src_ref=src, dst_ref=dst, send_sem=send, recv_sem=recv, device_id=to, device_id_type=MESH
    )


def hello(to):
    pl.semaphore_signal(pltpu.get_barrier_semaphore(), inc=1, device_id=to, device_id_type=MESH)


def meet(count):
    pl.semaphore_wait(pltpu.get_barrier_semaphore(), count)


def dot(a, b):
    return jnp.dot(a, b, precision=HI, preferred_element_type=F32)


def selection(meta):
    row = lax.broadcasted_iota(jnp.int32, (NB * G, TD * G), 0)
    lane = lax.broadcasted_iota(jnp.int32, (NB * G, TD * G), 1)
    first = meta[0:1, :].astype(jnp.int32)
    second = meta[1:2, :].astype(jnp.int32)
    flip = meta[2:3, :]
    bucket = row >> 3
    value = jnp.where(bucket == first, 1.0, 0.0) + jnp.where(bucket == second, flip, 0.0)
    return jnp.where((row & 7) == (lane & 7), value, 0.0).astype(BF16)


NBK = 64


def invert_block(block):
    n = NBK
    ident = (lax.broadcasted_iota(jnp.int32, (n, n), 0) == lax.broadcasted_iota(jnp.int32, (n, n), 1)).astype(F32)
    aug = jnp.concatenate([block, ident], axis=1)
    groups = n // G
    rows = [aug[g * G : (g + 1) * G, :] for g in range(groups)]
    sub = lax.broadcasted_iota(jnp.int32, (G, 2 * n), 0)
    for g in range(groups):
        cols = [
            {h: jnp.broadcast_to(rows[h][:, g * G + i : g * G + i + 1], (G, 2 * n)) for h in range(g, groups)}
            for i in range(G)
        ]
        scale = jnp.zeros((G, 2 * n), F32)
        for i in range(G):
            pivot = jnp.broadcast_to(cols[i][g][i : i + 1, :], (G, 2 * n))
            inv = 1.0 / pivot
            scale = jnp.where(sub == i, lax.rsqrt(pivot), scale)
            below = dict(cols[i])
            below[g] = jnp.where(sub > i, below[g], 0.0)
            for m in range(i + 1, G):
                f = jnp.broadcast_to(cols[m][g][i : i + 1, :], (G, 2 * n)) * inv
                for h in range(g, groups):
                    cols[m][h] = cols[m][h] - below[h] * f
            u = jnp.broadcast_to(rows[g][i : i + 1, :], (G, 2 * n)) * inv
            for h in range(g, groups):
                rows[h] = rows[h] - below[h] * u
        rows[g] = rows[g] * scale
    done = jnp.concatenate(rows, axis=0)
    return done[:, n:]


def start_factor(gram, work):
    work[:, :PS] = gram
    work[:, PS:] = (
        lax.broadcasted_iota(jnp.int32, (PS, PS), 0) == lax.broadcasted_iota(jnp.int32, (PS, PS), 1)
    ).astype(F32)


def factor_step(work, p):
    lo, hi = p * NBK, (p + 1) * NBK
    inv = invert_block(work[lo:hi, lo:hi])
    row = dot(inv, work[lo:hi, :])
    work[lo:hi, :] = row
    if hi < PS:
        work[hi:, :] = work[hi:, :] - dot(row[:, hi:PS].T, row)


VM = pl.BlockSpec(memory_space=pltpu.VMEM)
ANY = pl.BlockSpec(memory_space=pl.ANY)
DMA = pltpu.SemaphoreType.DMA
STEP_TILES = 8
QUARTER = PS // 4
OWN_ROWS = NB * G // NZ
TINY = 1e-30
FULL = 32767.0
FAR_FIRST = sorted(range(1, NZ), key=lambda d: -min(d, NZ - d))
RELAYS = ((4, (8, 5, 7)), (12, (14, 13, 15)), (1, (10, 9, 2)), (3, (6, 11)))


def to_code(value):
    return jnp.floor(value + 0.5).astype(jnp.int32).astype(jnp.int16)


def from_code(code):
    return code.astype(jnp.int32).astype(F32)


def top_of(value):
    return jnp.maximum(jnp.max(jnp.abs(value), axis=0, keepdims=True), TINY)


def mix_tiles(which, seeds, pairs, mat, mixers, m_ref, meta_ref):
    lane = lax.broadcasted_iota(jnp.int32, (1, TILE), 1) * 40503

    def some(step, carry):
        for pair in range(STEP_TILES // 2):
            parts = []
            for q in range(2):
                tile = step * STEP_TILES + 2 * pair + q
                hashed = (seeds[tile] ^ lane) * 69069
                sign = (1 - 2 * ((hashed >> 16) & 1)).astype(F32)
                mixer = mixers[which[tile]] * sign
                block = mat[pl.ds(pl.multiple_of(tile * TILE, TILE), TILE), :]
                parts.append(dot(mixer, block).reshape(TILE // G, G, mat.shape[1]))
            at = pl.multiple_of((step * STEP_TILES + 2 * pair) * G, 2 * G)
            m_ref[:, pl.ds(at, 2 * G), :] = jnp.concatenate(parts, axis=1).astype(BF16)
        return carry

    lax.fori_loop(0, TD // STEP_TILES, some, 0)
    tiles = lax.broadcasted_iota(jnp.int32, (1, TD * G), 1) // G
    first = jnp.zeros((1, TD * G), jnp.int32)
    second, seed = first, first
    for t in range(TD):
        first = jnp.where(tiles == t, pairs[0, t], first)
        second = jnp.where(tiles == t, pairs[1, t], second)
        seed = jnp.where(tiles == t, seeds[t], seed)
    flip = 1 - 2 * (seed >> 29 & 1)
    row = lax.broadcasted_iota(jnp.int32, (G, TD * G), 0)
    meta_ref[...] = jnp.where(row == 0, first, jnp.where(row == 1, second, flip)).astype(F32)


def main_kernel(
    which_in, seeds_in, pairs_in, mat_in, mixers_in, o_ref,
    which, seeds, pairs, mat, mixers, in_sems,
    m_ref, meta_ref, other_ref, x_ref, relay, y_ref, yq_ref, ys_ref, got_y, got_s, pq_ref, ps_ref,
    top_ref, got_t, w_ref, all_ref, g_ref, got_g, gram_ref, work, value, summed, pair, got_v,
    meta_sems, send_x, recv_x, send_r, recv_r,
    send_a, recv_a, send_b, recv_b, send_c, recv_c,
    send_as, recv_as, send_bs, recv_bs, send_cs, recv_cs, send_t, recv_t,
    send_w, recv_w, send_g, recv_g, send_h, recv_h,
    pair_sems, send_v, recv_v,
):
    z, k, x, y = place()
    col = x * NX + y
    source = col == 0
    sibling = {"k": 1 - k}

    def plane(d):
        other = lax.rem(k * NC + col + d, NK * NC)
        c = lax.rem(other, NC)
        return other // NC, c, {"k": other // NC, "x": c // NX, "y": lax.rem(c, NX)}

    def up(d):
        return lax.rem(z + d, NZ)

    for d in range(1, NK * NC):
        hello(plane(d)[2])
    for d in range(1, NZ):
        hello({"z": up(d)})
    loads = [
        pltpu.make_async_copy(src, dst, in_sems.at[i])
        for i, (src, dst) in enumerate(
            ((which_in, which), (seeds_in, seeds), (pairs_in, pairs), (mixers_in, mixers), (mat_in, mat))
        )
    ]
    for load in loads:
        load.start()
    for load in loads:
        load.wait()
    mix_tiles(which, seeds, pairs, mat, mixers, m_ref, meta_ref)
    meet(NK * NC - 1 + NZ - 1)

    sent = []

    def go(copy):
        copy.start()
        sent.append(copy)

    def landed(ref, recv):
        remote(ref, ref, send_x.at[0, 0], recv, sibling).wait_recv()

    def half(c, kd):
        return m_ref.at[c, :, kd * HALF : (kd + 1) * HALF]

    def spot(c):
        return {"x": c // NX, "y": c % NX}

    pieces = []
    for j in range(3):
        for first, rest in RELAYS:
            if j < len(rest):
                for kd in range(NK):
                    c = rest[j]
                    pieces.append((half(c, kd), relay.at[j, kd], send_x.at[c, kd], recv_r.at[j, kd], spot(first)))
    for first, rest in RELAYS:
        for kd in range(NK):
            pieces.append(
                (half(first, kd), x_ref.at[k], send_x.at[first, kd], recv_x.at[k], {"k": kd, **spot(first)})
            )
    cross_half = m_ref.at[0, :, pl.ds(pl.multiple_of((1 - k) * HALF, HALF), HALF)]
    pieces.append((cross_half, x_ref.at[k], send_x.at[0, 0], recv_x.at[k], sibling))

    @pl.when(source)
    def _():
        for piece in pieces:
            remote(*piece).start()
        x_ref[k] = jnp.where(k == 0, m_ref[0, :, :HALF], m_ref[0, :, HALF:])

    go(remote(meta_ref, other_ref, meta_sems.at[0], meta_sems.at[1], sibling))

    def onward(j, kd, c):
        return remote(relay.at[j, kd], x_ref.at[k], send_r.at[j, kd], recv_x.at[k], {"k": kd, **spot(c)})

    for first, rest in RELAYS:
        @pl.when(col == first)
        def _():
            for j, c in enumerate(rest):
                for kd in range(NK):
                    landed(relay.at[j, kd], recv_r.at[j, kd])
                    onward(j, kd, c).start()

    landed(other_ref, meta_sems.at[1])
    mine = selection(meta_ref[...])
    theirs = selection(other_ref[...])

    @pl.when(jnp.logical_not(source))
    def _():
        landed(x_ref.at[k], recv_x.at[k])

    landed(x_ref.at[1 - k], recv_x.at[1 - k])
    part = jnp.dot(mine, x_ref[k], preferred_element_type=F32)
    part = part + jnp.dot(theirs, x_ref[1 - k], preferred_element_type=F32)
    y_ref[...] = part.reshape(y_ref.shape)
    top = top_of(part)
    yq_ref[...] = to_code(part * (FULL / top)).reshape(yq_ref.shape)
    ys_ref[...] = top * (1.0 / FULL)

    for d in FAR_FIRST:
        go(remote(yq_ref.at[up(d)], got_y.at[d - 1], send_a.at[d - 1], recv_a.at[d - 1], {"z": up(d)}))
        go(remote(ys_ref, got_s.at[d - 1], send_as.at[d - 1], recv_as.at[d - 1], {"z": up(d)}))
    acc = y_ref[z]
    for d in FAR_FIRST[::-1]:
        landed(got_y.at[d - 1], recv_a.at[d - 1])
        landed(got_s.at[d - 1], recv_as.at[d - 1])
        acc = acc + from_code(got_y[d - 1]) * got_s[d - 1]
    top = top_of(acc)
    pq_ref[k, z] = to_code(acc * (FULL / top))
    ps_ref[k, z] = top * (1.0 / FULL)

    def both(kk, zs, i, sems, scale_sems, to):
        go(remote(pq_ref.at[kk, zs], pq_ref.at[kk, zs], sems[0].at[i], sems[1].at[i], to))
        go(remote(ps_ref.at[kk, zs], ps_ref.at[kk, zs], scale_sems[0].at[i], scale_sems[1].at[i], to))

    for d in FAR_FIRST:
        both(k, z, d - 1, (send_b, recv_b), (send_bs, recv_bs), {"z": up(d)})
    both(k, z, 0, (send_c, recv_c), (send_cs, recv_cs), sibling)
    for d in FAR_FIRST[::-1]:
        zs = up(NZ - d)
        landed(pq_ref.at[k, zs], recv_b.at[d - 1])
        landed(ps_ref.at[k, zs], recv_bs.at[d - 1])
        both(k, zs, d, (send_c, recv_c), (send_cs, recv_cs), sibling)
    for d in [0] + FAR_FIRST[::-1]:
        landed(pq_ref.at[1 - k, up(NZ - d)], recv_c.at[d])
        landed(ps_ref.at[1 - k, up(NZ - d)], recv_cs.at[d])

    sketch = jnp.concatenate(
        [(from_code(pq_ref[kk]) * ps_ref[kk]).reshape(NB * G, HALF) for kk in range(NK)], axis=1
    )
    top_ref[...] = top_of(sketch)

    def same_core(d):
        c = lax.rem(col + d, NC)
        return {"x": c // NX, "y": lax.rem(c, NX)}

    for d in range(1, NC):
        go(remote(top_ref, got_t.at[d - 1], send_t.at[d - 1], recv_t.at[d - 1], same_core(d)))
    turned = sketch.T
    g_ref[...] = dot(turned, sketch)

    def rows_of(kk, c):
        return pl.ds(pl.multiple_of(kk * HALF + c * G, G), G)

    for d in range(1, NC):
        go(remote(g_ref.at[rows_of(k, lax.rem(col + d, NC)), :], got_g.at[d - 1], send_g.at[d - 1], recv_g.at[d - 1], same_core(d)))
    weight = dot(turned, mine.astype(F32))
    top = top_ref[...]
    for d in range(1, NC):
        landed(got_t.at[d - 1], recv_t.at[d - 1])
        top = jnp.maximum(top, got_t[d - 1])
    unit = top * (2.0 / (FULL - 1.0))
    inverse = jnp.broadcast_to(1.0 / unit, (G, PS)).T[:, 0:1]
    w_ref[...] = to_code(weight * inverse)

    def piece_of(h, s):
        return pl.ds((2 * h + s) * QUARTER, QUARTER)

    def index(h, a, b):
        if h == 0:
            return lax.rem(x + a, NX) * NX + lax.rem(y + b, NX)
        return lax.rem(x + b, NX) * NX + lax.rem(y + a, NX)

    def send(h, a, b, s, stage, direction):
        c = index(h, a, b)
        there = all_ref.at[c, piece_of(h, s), :]
        here = w_ref.at[piece_of(h, s), :] if a == b == 0 else there
        step = 1 if direction == 0 else NX - 1
        to = {"x": lax.rem(x + step, NX)} if (h == 0) == (stage == 0) else {"y": lax.rem(y + step, NX)}
        go(remote(here, there, send_w.at[h, c, s, stage, direction], recv_w.at[h, c, s], to))

    seen = {(h, 0, 0, s) for h in range(2) for s in range(2)}

    def arrived(h, a, b, s):
        if (h, a, b, s) not in seen:
            seen.add((h, a, b, s))
            c = index(h, a, b)
            landed(all_ref.at[c, piece_of(h, s), :], recv_w.at[h, c, s])

    def across(h, a, s):
        arrived(h, a, 0, s)
        send(h, a, 0, s, 1, s)
        send(h, a, 0, s, 1, 1 - s)

    def pass_on(a):
        for h in range(2):
            arrived(h, a, 3, 0)
            send(h, a, 3, 0, 1, 0)
            arrived(h, a, 1, 1)
            send(h, a, 1, 1, 1, 1)

    for stage in range(2):
        for turn in range(2):
            for s in range(2):
                for h in range(2):
                    send(h, 0, 0, s, stage, s if turn == 0 else 1 - s)

    acc = g_ref[rows_of(k, col), :]
    for d in range(1, NC):
        landed(got_g.at[d - 1], recv_g.at[d - 1])
        acc = acc + got_g[d - 1]
    gram_ref[rows_of(k, col), :] = acc
    for d in range(1, NK * NC):
        own = gram_ref.at[rows_of(k, col), :]
        go(remote(own, own, send_h.at[d - 1], recv_h.at[d - 1], plane(d)[2]))

    for h in range(2):
        arrived(h, 3, 0, 0)
        send(h, 3, 0, 0, 0, 0)
        arrived(h, 1, 0, 1)
        send(h, 1, 0, 1, 0, 1)
    for a, s in ((3, 0), (1, 1), (3, 1), (1, 0)):
        for h in range(2):
            across(h, a, s)
    for d in range(1, NK * NC):
        kk, c, _ = plane(NK * NC - d)
        landed(gram_ref.at[rows_of(kk, c), :], recv_h.at[d - 1])
    all_ref[col] = w_ref[...]
    start_factor(gram_ref[...], work)
    factor_step(work, 0)
    for h in range(2):
        for s in range(2):
            across(h, 2, s)
    pass_on(0)
    factor_step(work, 1)
    pass_on(3)
    pass_on(1)
    factor_step(work, 2)
    pass_on(2)
    factor_step(work, 3)

    def ready(dx, dy):
        for s in range(2):
            arrived(0, dx, dy, s)
            arrived(1, dy, dx, s)

    def add(dx, dy, acc):
        c = lax.rem(x + dx, NX) * NX + lax.rem(y + dy, NX)
        w = from_code(all_ref[c])
        high = w.astype(BF16)
        low = (w - high.astype(F32)).astype(BF16)
        tiles = m_ref[c]
        for part in (high, low):
            acc = acc + jnp.dot(part, tiles, preferred_element_type=F32)
        return acc

    cross = jnp.zeros((PS, m_ref.shape[2]), F32)
    for d in range(NX):
        ready(d, 0)
        ready(0, d)
    cross = lax.fori_loop(
        0, 2 * NX - 1, lambda j, acc: add(jnp.where(j < NX, j, 0), jnp.where(j < NX, 0, j - NX + 1), acc), cross
    )
    for dx in range(1, NX):
        for dy in range(1, NX):
            ready(dx, dy)
    cross = lax.fori_loop(0, (NX - 1) ** 2, lambda j, acc: add(1 + j // 3, 1 + lax.rem(j, 3), acc), cross)
    value[...] = dot(work[:, PS:] * unit, cross).reshape(value.shape)
    go(remote(value.at[:, 1 - k], pair, pair_sems.at[0], pair_sems.at[1], sibling))
    landed(pair, pair_sems.at[1])
    summed[...] = value[:, k] + pair[...]
    for d in FAR_FIRST:
        go(remote(summed.at[up(d)], got_v.at[d - 1], send_v.at[d - 1], recv_v.at[d - 1], {"z": up(d)}))
    acc = summed[z]
    for d in FAR_FIRST[::-1]:
        landed(got_v.at[d - 1], recv_v.at[d - 1])
        acc = acc + got_v[d - 1]
    o_ref[...] = acc

    @pl.when(source)
    def _():
        for piece in pieces:
            remote(*piece).wait_send()

    for first, rest in RELAYS:
        @pl.when(col == first)
        def _():
            for j, c in enumerate(rest):
                for kd in range(NK):
                    onward(j, kd, c).wait_send()

    for copy in sent:
        copy.wait_send()


def local(matrix, mixers, bucket_pair, mixer_index, sign_seed):
    width = matrix.shape[1]
    one, two, plane = (NZ - 1,), (2,), (NK * NC - 1,)
    return pl.pallas_call(
        main_kernel,
        out_shape=jax.ShapeDtypeStruct((G, width), F32),
        in_specs=[ANY] * 5,
        out_specs=VM,
        scratch_shapes=[
            pltpu.SMEM((TD,), jnp.int32),
            pltpu.SMEM((TD,), jnp.int32),
            pltpu.SMEM((2, TD), jnp.int32),
            pltpu.VMEM(matrix.shape, F32),
            pltpu.VMEM(mixers.shape, F32),
            DMA((5,)),
            pltpu.VMEM((NC, TD * G, width), BF16),
            pltpu.VMEM((G, TD * G), F32),
            pltpu.VMEM((G, TD * G), F32),
            pltpu.VMEM((NK, TD * G, HALF), BF16),
            pltpu.VMEM((3, NK, TD * G, HALF), BF16),
            pltpu.VMEM((NZ, OWN_ROWS, HALF), F32),
            pltpu.VMEM((NZ, OWN_ROWS, HALF), jnp.int16),
            pltpu.VMEM((1, HALF), F32),
            pltpu.VMEM((NZ - 1, OWN_ROWS, HALF), jnp.int16),
            pltpu.VMEM((NZ - 1, 1, HALF), F32),
            pltpu.VMEM((NK, NZ, OWN_ROWS, HALF), jnp.int16),
            pltpu.VMEM((NK, NZ, 1, HALF), F32),
            pltpu.VMEM((1, PS), F32),
            pltpu.VMEM((NC - 1, 1, PS), F32),
            pltpu.VMEM((PS, TD * G), jnp.int16),
            pltpu.VMEM((NC, PS, TD * G), jnp.int16),
            pltpu.VMEM((PS, PS), F32),
            pltpu.VMEM((NC - 1, G, PS), F32),
            pltpu.VMEM((PS, PS), F32),
            pltpu.VMEM((PS, 2 * PS), F32),
            pltpu.VMEM((NZ, NK, G, width), F32),
            pltpu.VMEM((NZ, G, width), F32),
            pltpu.VMEM((NZ, G, width), F32),
            pltpu.VMEM((NZ - 1, G, width), F32),
            DMA(two), DMA((NC, NK)), DMA(two), DMA((3, NK)), DMA((3, NK)),
            DMA(one), DMA(one), DMA(one), DMA(one), DMA((NZ,)), DMA((NZ,)),
            DMA(one), DMA(one), DMA(one), DMA(one), DMA((NZ,)), DMA((NZ,)), DMA((NC - 1,)), DMA((NC - 1,)),
            DMA((2, NC, 2, 2, 2)), DMA((2, NC, 2)), DMA((NC - 1,)), DMA((NC - 1,)), DMA(plane), DMA(plane),
            DMA(two), DMA(one), DMA(one),
        ],
        compiler_params=pltpu.CompilerParams(collective_id=1, has_side_effects=True),
        name="main",
    )(mixer_index, sign_seed, bucket_pair.T, matrix, mixers)


def solution(mesh):
    split = Mesh(mesh.devices.reshape(NZ, NK, NX, NX), ("z", "k", "x", "y"))
    return jax.shard_map(
        local,
        mesh=split,
        in_specs=(P(ROWS, COLS), P(), P(ROWS, None), P(ROWS), P(ROWS)),
        out_specs=P(ROWS, COLS),
        check_vma=False,
    )
```

```python
import functools

import jax
import jax.numpy as jnp
from jax import lax
from jax.experimental import pallas as pl
from jax.experimental.pallas import tpu as pltpu
from jax.sharding import Mesh
from jax.sharding import PartitionSpec as P

TILE = 128
PS = 256
NB = 64
TD = 32
NZ = 16
NK = 2
NX = 4
NC = 16
G = 8
HALF = 128
MESH = pl.DeviceIdType.MESH
HI = lax.Precision.HIGHEST
ROWS = ("z", "k")
COLS = ("x", "y")
F32 = jnp.float32
BF16 = jnp.bfloat16


def place():
    return tuple(lax.axis_index(a) for a in ("z", "k", "x", "y"))


def remote(src, dst, send, recv, to):
    return pltpu.make_async_remote_copy(
        src_ref=src, dst_ref=dst, send_sem=send, recv_sem=recv, device_id=to, device_id_type=MESH
    )


def hello(to):
    pl.semaphore_signal(pltpu.get_barrier_semaphore(), inc=1, device_id=to, device_id_type=MESH)


def meet(count):
    pl.semaphore_wait(pltpu.get_barrier_semaphore(), count)


def dot(a, b):
    return jnp.dot(a, b, precision=HI, preferred_element_type=F32)


def selection(meta):
    row = lax.broadcasted_iota(jnp.int32, (NB * G, TD * G), 0)
    lane = lax.broadcasted_iota(jnp.int32, (NB * G, TD * G), 1)
    first = meta[0:1, :].astype(jnp.int32)
    second = meta[1:2, :].astype(jnp.int32)
    flip = meta[2:3, :]
    bucket = row >> 3
    value = jnp.where(bucket == first, 1.0, 0.0) + jnp.where(bucket == second, flip, 0.0)
    return jnp.where((row & 7) == (lane & 7), value, 0.0).astype(BF16)


NBK = 64


def invert_block(block):
    n = NBK
    ident = (lax.broadcasted_iota(jnp.int32, (n, n), 0) == lax.broadcasted_iota(jnp.int32, (n, n), 1)).astype(F32)
    aug = jnp.concatenate([block, ident], axis=1)
    groups = n // G
    rows = [aug[g * G : (g + 1) * G, :] for g in range(groups)]
    sub = lax.broadcasted_iota(jnp.int32, (G, 2 * n), 0)
    for g in range(groups):
        cols = [
            {h: jnp.broadcast_to(rows[h][:, g * G + i : g * G + i + 1], (G, 2 * n)) for h in range(g, groups)}
            for i in range(G)
        ]
        scale = jnp.zeros((G, 2 * n), F32)
        for i in range(G):
            pivot = jnp.broadcast_to(cols[i][g][i : i + 1, :], (G, 2 * n))
            inv = 1.0 / pivot
            scale = jnp.where(sub == i, lax.rsqrt(pivot), scale)
            below = dict(cols[i])
            below[g] = jnp.where(sub > i, below[g], 0.0)
            for m in range(i + 1, G):
                f = jnp.broadcast_to(cols[m][g][i : i + 1, :], (G, 2 * n)) * inv
                for h in range(g, groups):
                    cols[m][h] = cols[m][h] - below[h] * f
            u = jnp.broadcast_to(rows[g][i : i + 1, :], (G, 2 * n)) * inv
            for h in range(g, groups):
                rows[h] = rows[h] - below[h] * u
        rows[g] = rows[g] * scale
    done = jnp.concatenate(rows, axis=0)
    return done[:, n:]


def start_factor(gram, work):
    work[:, :PS] = gram
    work[:, PS:] = (
        lax.broadcasted_iota(jnp.int32, (PS, PS), 0) == lax.broadcasted_iota(jnp.int32, (PS, PS), 1)
    ).astype(F32)


def factor_step(work, p):
    lo, hi = p * NBK, (p + 1) * NBK
    inv = invert_block(work[lo:hi, lo:hi])
    left, right = lo // HALF * HALF, PS + -(-hi // HALF) * HALF
    row = dot(inv, work[lo:hi, left:right])
    work[lo:hi, left:right] = row
    if hi < PS:
        work[hi:, left:right] = work[hi:, left:right] - dot(row[:, hi - left : PS - left].T, row)


VM = pl.BlockSpec(memory_space=pltpu.VMEM)
ANY = pl.BlockSpec(memory_space=pl.ANY)
DMA = pltpu.SemaphoreType.DMA
STEP_TILES = 8
QUARTER = PS // 4
OWN_ROWS = NB * G // NZ
TINY = 1e-30
FULL = 32767.0
FAR_FIRST = sorted(range(1, NZ), key=lambda d: -min(d, NZ - d))
RELAYS = ((4, (8, 5, 7)), (12, (14, 13, 15)), (1, (10, 9, 2)), (3, (6, 11)))


def to_code(value):
    return jnp.floor(value + 0.5).astype(jnp.int32).astype(jnp.int16)


def from_code(code):
    return code.astype(jnp.int32).astype(F32)


def top_of(value):
    return jnp.maximum(jnp.max(jnp.abs(value), axis=0, keepdims=True), TINY)


def mix_tiles(which, seeds, mat, mixers, m_ref, part):
    lane = lax.broadcasted_iota(jnp.int32, (1, TILE), 1) * 40503

    def some(step, carry):
        for pair in range(STEP_TILES // 2):
            parts = []
            for q in range(2):
                tile = step * STEP_TILES + 2 * pair + q
                hashed = (seeds[tile] ^ lane) * 69069
                sign = (1 - 2 * ((hashed >> 16) & 1)).astype(F32)
                mixer = mixers[which[tile]] * sign
                block = mat[pl.ds(pl.multiple_of(tile * TILE, TILE), TILE), :]
                parts.append(dot(mixer, block).reshape(TILE // G, G, mat.shape[1]))
            at = pl.multiple_of((step * STEP_TILES + 2 * pair) * G, 2 * G)
            m_ref[:, pl.ds(at, 2 * G), :] = jnp.concatenate(parts, axis=1).astype(BF16)
        return carry

    steps = TD // STEP_TILES // 2
    lax.fori_loop(part * steps, (part + 1) * steps, some, 0)


def fill_meta(seeds, pairs, meta_ref):
    tiles = lax.broadcasted_iota(jnp.int32, (1, TD * G), 1) // G
    first = jnp.zeros((1, TD * G), jnp.int32)
    second, seed = first, first
    for t in range(TD):
        first = jnp.where(tiles == t, pairs[0, t], first)
        second = jnp.where(tiles == t, pairs[1, t], second)
        seed = jnp.where(tiles == t, seeds[t], seed)
    flip = 1 - 2 * (seed >> 29 & 1)
    row = lax.broadcasted_iota(jnp.int32, (G, TD * G), 0)
    meta_ref[...] = jnp.where(row == 0, first, jnp.where(row == 1, second, flip)).astype(F32)


def main_kernel(
    which_in, seeds_in, pairs_in, mat_in, mixers_in, o_ref,
    which, seeds, pairs, mat, mixers, in_sems,
    m_ref, meta_ref, other_ref, x_ref, relay, y_ref, yq_ref, ys_ref, got_y, pq_ref, ps_ref,
    top_ref, got_t, w_ref, all_ref, g_ref, got_g, gram_ref, work, value, summed, pair, got_v,
    meta_sems, send_x, recv_x, send_r, recv_r,
    send_a, recv_a, send_b, recv_b, send_c, recv_c,
    send_as, recv_as, send_bs, recv_bs, send_t, recv_t,
    send_w, recv_w, send_g, recv_g, send_h, recv_h,
    pair_sems, send_v, recv_v,
):
    z, k, x, y = place()
    col = x * NX + y
    source = col == 0
    sibling = {"k": 1 - k}

    def plane(d):
        other = lax.rem(k * NC + col + d, NK * NC)
        c = lax.rem(other, NC)
        return other // NC, c, {"k": other // NC, "x": c // NX, "y": lax.rem(c, NX)}

    def up(d):
        return lax.rem(z + d, NZ)

    rows = TD * TILE // 2
    loads = [
        pltpu.make_async_copy(src, dst, in_sems.at[i])
        for i, (src, dst) in enumerate(
            (
                (which_in, which),
                (seeds_in, seeds),
                (pairs_in, pairs),
                (mixers_in, mixers),
                (mat_in.at[:rows, :], mat.at[:rows, :]),
                (mat_in.at[rows:, :], mat.at[rows:, :]),
            )
        )
    ]
    for load in loads:
        load.start()
    for d in FAR_FIRST:
        hello({"z": up(d)})
    for d in range(1, NK * NC):
        hello(plane(d)[2])
    for load in loads[:-1]:
        load.wait()
    mix_tiles(which, seeds, mat, mixers, m_ref, 0)
    fill_meta(seeds, pairs, meta_ref)
    meet(NK * NC - 1 + NZ - 1)

    sent = []

    def go(copy):
        copy.start()
        sent.append(copy)

    def landed(ref, recv):
        remote(ref, ref, send_x.at[0, 0, 0], recv, sibling).wait_recv()

    part_rows = TD * G // 2

    def rows_in(part):
        return pl.ds(part * part_rows, part_rows)

    def half(c, kd, part):
        return m_ref.at[c, rows_in(part), kd * HALF : (kd + 1) * HALF]

    def home(part):
        return x_ref.at[k, rows_in(part), :]

    def spot(c):
        return {"x": c // NX, "y": c % NX}

    pieces = ([], [])
    for part in range(2):
        for j in range(3):
            for first, rest in RELAYS:
                if j < len(rest):
                    for kd in range(NK):
                        c = rest[j]
                        pieces[part].append(
                            (half(c, kd, part), relay.at[j, kd, rows_in(part), :], send_x.at[c, kd, part],
                             recv_r.at[j, kd, part], spot(first))
                        )
        for first, rest in RELAYS:
            for kd in range(NK):
                pieces[part].append(
                    (half(first, kd, part), home(part), send_x.at[first, kd, part], recv_x.at[k, part],
                     {"k": kd, **spot(first)})
                )
        cross_half = m_ref.at[0, rows_in(part), pl.ds(pl.multiple_of((1 - k) * HALF, HALF), HALF)]
        pieces[part].append((cross_half, home(part), send_x.at[0, 0, part], recv_x.at[k, part], sibling))

    @pl.when(source)
    def _():
        for piece in pieces[0]:
            remote(*piece).start()

    go(remote(meta_ref, other_ref, meta_sems.at[0], meta_sems.at[1], sibling))
    loads[-1].wait()
    mix_tiles(which, seeds, mat, mixers, m_ref, 1)

    @pl.when(source)
    def _():
        for piece in pieces[1]:
            remote(*piece).start()
        x_ref[k] = jnp.where(k == 0, m_ref[0, :, :HALF], m_ref[0, :, HALF:])

    def onward(j, kd, part, c):
        return remote(
            relay.at[j, kd, rows_in(part), :], home(part), send_r.at[j, kd, part], recv_x.at[k, part],
            {"k": kd, **spot(c)}
        )

    for first, rest in RELAYS:
        @pl.when(col == first)
        def _():
            for part in range(2):
                for j, c in enumerate(rest):
                    for kd in range(NK):
                        landed(relay.at[j, kd, rows_in(part), :], recv_r.at[j, kd, part])
                        onward(j, kd, part, c).start()

    landed(other_ref, meta_sems.at[1])
    mine = selection(meta_ref[...])
    theirs = selection(other_ref[...])

    part = jnp.zeros((NB * G, HALF), F32)
    for p in range(2):
        @pl.when(jnp.logical_not(source))
        def _():
            landed(x_ref.at[k, rows_in(p), :], recv_x.at[k, p])

        landed(x_ref.at[1 - k, rows_in(p), :], recv_x.at[1 - k, p])
        span = slice(p * part_rows, (p + 1) * part_rows)
        part = part + jnp.dot(mine[:, span], x_ref[k, span, :], preferred_element_type=F32)
        part = part + jnp.dot(theirs[:, span], x_ref[1 - k, span, :], preferred_element_type=F32)
    y_ref[...] = part.reshape(y_ref.shape)
    top = top_of(part)
    yq_ref[...] = to_code(part * (FULL / top)).reshape(yq_ref.shape)
    ys_ref[z] = top

    for d in FAR_FIRST:
        go(remote(yq_ref.at[up(d)], got_y.at[d - 1], send_a.at[d - 1], recv_a.at[d - 1], {"z": up(d)}))
        go(remote(ys_ref.at[z], ys_ref.at[z], send_as.at[d - 1], recv_as.at[d - 1], {"z": up(d)}))
    acc = y_ref[z]
    for d in FAR_FIRST[::-1]:
        zs = up(NZ - d)
        landed(got_y.at[d - 1], recv_a.at[d - 1])
        landed(ys_ref.at[zs], recv_as.at[d - 1])
        acc = acc + from_code(got_y[d - 1]) * (ys_ref[zs] * (1.0 / FULL))
    top = ys_ref[0]
    for other_z in range(1, NZ):
        top = top + ys_ref[other_z]
    top = top * 1.00001
    pq_ref[k, z] = to_code(acc * (FULL / top))
    ps_ref[k] = top * (1.0 / FULL)
    go(remote(ps_ref.at[k], ps_ref.at[k], send_bs, recv_bs, sibling))

    for d in FAR_FIRST:
        go(remote(pq_ref.at[k, z], pq_ref.at[k, z], send_b.at[d - 1], recv_b.at[d - 1], {"z": up(d)}))
    go(remote(pq_ref.at[k, z], pq_ref.at[k, z], send_c.at[0], recv_c.at[0], sibling))
    for d in FAR_FIRST[::-1]:
        zs = up(NZ - d)
        landed(pq_ref.at[k, zs], recv_b.at[d - 1])
        go(remote(pq_ref.at[k, zs], pq_ref.at[k, zs], send_c.at[d], recv_c.at[d], sibling))
    landed(ps_ref.at[1 - k], recv_bs)
    for d in [0] + FAR_FIRST[::-1]:
        landed(pq_ref.at[1 - k, up(NZ - d)], recv_c.at[d])

    sketch = jnp.concatenate(
        [from_code(pq_ref[kk]).reshape(NB * G, HALF) * ps_ref[kk] for kk in range(NK)], axis=1
    )
    top_ref[...] = top_of(sketch)

    def same_core(d):
        c = lax.rem(col + d, NC)
        return {"x": c // NX, "y": lax.rem(c, NX)}

    for d in range(1, NC):
        go(remote(top_ref, got_t.at[d - 1], send_t.at[d - 1], recv_t.at[d - 1], same_core(d)))
    turned = sketch.T
    g_ref[...] = dot(turned, sketch)

    def rows_of(kk, c):
        return pl.ds(pl.multiple_of(kk * HALF + c * G, G), G)

    for d in range(1, NC):
        go(remote(g_ref.at[rows_of(k, lax.rem(col + d, NC)), :], got_g.at[d - 1], send_g.at[d - 1], recv_g.at[d - 1], same_core(d)))
    weight = dot(turned, mine.astype(F32))
    top = top_ref[...]
    for d in range(1, NC):
        landed(got_t.at[d - 1], recv_t.at[d - 1])
        top = jnp.maximum(top, got_t[d - 1])
    unit = top * (2.0 / (FULL - 1.0))
    inverse = jnp.broadcast_to(1.0 / unit, (G, PS)).T[:, 0:1]
    w_ref[...] = to_code(weight * inverse)

    def piece_of(h, s):
        return pl.ds((2 * h + s) * QUARTER, QUARTER)

    def index(h, a, b):
        if h == 0:
            return lax.rem(x + a, NX) * NX + lax.rem(y + b, NX)
        return lax.rem(x + b, NX) * NX + lax.rem(y + a, NX)

    def send(h, a, b, s, stage, direction):
        c = index(h, a, b)
        there = all_ref.at[c, piece_of(h, s), :]
        here = w_ref.at[piece_of(h, s), :] if a == b == 0 else there
        step = 1 if direction == 0 else NX - 1
        to = {"x": lax.rem(x + step, NX)} if (h == 0) == (stage == 0) else {"y": lax.rem(y + step, NX)}
        go(remote(here, there, send_w.at[h, c, s, stage, direction], recv_w.at[h, c, s], to))

    seen = {(h, 0, 0, s) for h in range(2) for s in range(2)}

    def arrived(h, a, b, s):
        if (h, a, b, s) not in seen:
            seen.add((h, a, b, s))
            c = index(h, a, b)
            landed(all_ref.at[c, piece_of(h, s), :], recv_w.at[h, c, s])

    def across(h, a, s):
        arrived(h, a, 0, s)
        send(h, a, 0, s, 1, s)
        send(h, a, 0, s, 1, 1 - s)

    def pass_on(a):
        for h in range(2):
            arrived(h, a, 3, 0)
            send(h, a, 3, 0, 1, 0)
            arrived(h, a, 1, 1)
            send(h, a, 1, 1, 1, 1)

    def own_blocks(stage):
        for turn in range(2):
            for s in range(2):
                for h in range(2):
                    send(h, 0, 0, s, stage, s if turn == 0 else 1 - s)

    own_blocks(0)
    acc = g_ref[rows_of(k, col), :]
    for d in range(1, NC):
        landed(got_g.at[d - 1], recv_g.at[d - 1])
        acc = acc + got_g[d - 1]
    gram_ref[rows_of(k, col), :] = acc
    for d in range(1, NK * NC):
        own = gram_ref.at[rows_of(k, col), :]
        go(remote(own, own, send_h.at[d - 1], recv_h.at[d - 1], plane(d)[2]))
    own_blocks(1)

    for h in range(2):
        arrived(h, 3, 0, 0)
        send(h, 3, 0, 0, 0, 0)
        arrived(h, 1, 0, 1)
        send(h, 1, 0, 1, 0, 1)
    for a, s in ((3, 0), (1, 1), (3, 1), (1, 0)):
        for h in range(2):
            across(h, a, s)
    for d in range(1, NK * NC):
        kk, c, _ = plane(NK * NC - d)
        landed(gram_ref.at[rows_of(kk, c), :], recv_h.at[d - 1])
    all_ref[col] = w_ref[...]
    start_factor(gram_ref[...], work)
    factor_step(work, 0)
    for h in range(2):
        for s in range(2):
            across(h, 2, s)
    pass_on(0)
    factor_step(work, 1)
    pass_on(3)
    pass_on(1)
    factor_step(work, 2)
    pass_on(2)
    factor_step(work, 3)

    def ready(dx, dy):
        for s in range(2):
            arrived(0, dx, dy, s)
            arrived(1, dy, dx, s)

    def add(dx, dy, acc):
        c = lax.rem(x + dx, NX) * NX + lax.rem(y + dy, NX)
        w = from_code(all_ref[c])
        high = w.astype(BF16)
        low = (w - high.astype(F32)).astype(BF16)
        tiles = m_ref[c]
        for part in (high, low):
            acc = acc + jnp.dot(part, tiles, preferred_element_type=F32)
        return acc

    cross = jnp.zeros((PS, m_ref.shape[2]), F32)
    for d in range(NX):
        ready(d, 0)
        ready(0, d)
    cross = lax.fori_loop(
        0, 2 * NX - 1, lambda j, acc: add(jnp.where(j < NX, j, 0), jnp.where(j < NX, 0, j - NX + 1), acc), cross
    )
    for offsets in (((1, 1), (1, 3), (3, 1), (3, 3)), ((1, 2), (3, 2), (2, 1), (2, 3)), ((2, 2),)):
        for dx, dy in offsets:
            ready(dx, dy)
        for dx, dy in offsets:
            cross = add(dx, dy, cross)
    value[...] = dot(work[:, PS:] * unit, cross).reshape(value.shape)
    go(remote(value.at[:, 1 - k], pair, pair_sems.at[0], pair_sems.at[1], sibling))
    landed(pair, pair_sems.at[1])
    summed[...] = value[:, k] + pair[...]
    for d in FAR_FIRST:
        go(remote(summed.at[up(d)], got_v.at[d - 1], send_v.at[d - 1], recv_v.at[d - 1], {"z": up(d)}))
    acc = summed[z]
    for d in FAR_FIRST[::-1]:
        landed(got_v.at[d - 1], recv_v.at[d - 1])
        acc = acc + got_v[d - 1]
    o_ref[...] = acc

    @pl.when(source)
    def _():
        for piece in pieces[0] + pieces[1]:
            remote(*piece).wait_send()

    for first, rest in RELAYS:
        @pl.when(col == first)
        def _():
            for part in range(2):
                for j, c in enumerate(rest):
                    for kd in range(NK):
                        onward(j, kd, part, c).wait_send()

    for copy in sent:
        copy.wait_send()


def local(matrix, mixers, bucket_pair, mixer_index, sign_seed):
    width = matrix.shape[1]
    one, two, plane = (NZ - 1,), (2,), (NK * NC - 1,)
    return pl.pallas_call(
        main_kernel,
        out_shape=jax.ShapeDtypeStruct((G, width), F32),
        in_specs=[ANY] * 5,
        out_specs=VM,
        scratch_shapes=[
            pltpu.SMEM((TD,), jnp.int32),
            pltpu.SMEM((TD,), jnp.int32),
            pltpu.SMEM((2, TD), jnp.int32),
            pltpu.VMEM(matrix.shape, F32),
            pltpu.VMEM(mixers.shape, F32),
            DMA((6,)),
            pltpu.VMEM((NC, TD * G, width), BF16),
            pltpu.VMEM((G, TD * G), F32),
            pltpu.VMEM((G, TD * G), F32),
            pltpu.VMEM((NK, TD * G, HALF), BF16),
            pltpu.VMEM((3, NK, TD * G, HALF), BF16),
            pltpu.VMEM((NZ, OWN_ROWS, HALF), F32),
            pltpu.VMEM((NZ, OWN_ROWS, HALF), jnp.int16),
            pltpu.VMEM((NZ, 1, HALF), F32),
            pltpu.VMEM((NZ - 1, OWN_ROWS, HALF), jnp.int16),
            pltpu.VMEM((NK, NZ, OWN_ROWS, HALF), jnp.int16),
            pltpu.VMEM((NK, 1, HALF), F32),
            pltpu.VMEM((1, PS), F32),
            pltpu.VMEM((NC - 1, 1, PS), F32),
            pltpu.VMEM((PS, TD * G), jnp.int16),
            pltpu.VMEM((NC, PS, TD * G), jnp.int16),
            pltpu.VMEM((PS, PS), F32),
            pltpu.VMEM((NC - 1, G, PS), F32),
            pltpu.VMEM((PS, PS), F32),
            pltpu.VMEM((PS, 2 * PS), F32),
            pltpu.VMEM((NZ, NK, G, width), F32),
            pltpu.VMEM((NZ, G, width), F32),
            pltpu.VMEM((NZ, G, width), F32),
            pltpu.VMEM((NZ - 1, G, width), F32),
            DMA(two), DMA((NC, NK, 2)), DMA((NK, 2)), DMA((3, NK, 2)), DMA((3, NK, 2)),
            DMA(one), DMA(one), DMA(one), DMA(one), DMA((NZ,)), DMA((NZ,)),
            DMA(one), DMA(one), DMA, DMA, DMA((NC - 1,)), DMA((NC - 1,)),
            DMA((2, NC, 2, 2, 2)), DMA((2, NC, 2)), DMA((NC - 1,)), DMA((NC - 1,)), DMA(plane), DMA(plane),
            DMA(two), DMA(one), DMA(one),
        ],
        compiler_params=pltpu.CompilerParams(collective_id=1, has_side_effects=True),
        name="main",
    )(mixer_index, sign_seed, bucket_pair.T, matrix, mixers)


def solution(mesh):
    split = Mesh(mesh.devices.reshape(NZ, NK, NX, NX), ("z", "k", "x", "y"))
    return jax.shard_map(
        local,
        mesh=split,
        in_specs=(P(ROWS, COLS), P(), P(ROWS, None), P(ROWS), P(ROWS)),
        out_specs=P(ROWS, COLS),
        check_vma=False,
    )
```

```python
import functools

import jax
import jax.numpy as jnp
from jax import lax
from jax.experimental import pallas as pl
from jax.experimental.pallas import tpu as pltpu
from jax.sharding import Mesh
from jax.sharding import PartitionSpec as P

TILE = 128
PS = 256
NB = 64
TD = 32
NZ = 16
NK = 2
NX = 4
NC = 16
G = 8
HALF = 128
MESH = pl.DeviceIdType.MESH
HI = lax.Precision.HIGHEST
ROWS = ("z", "k")
COLS = ("x", "y")
F32 = jnp.float32
BF16 = jnp.bfloat16


def place():
    return tuple(lax.axis_index(a) for a in ("z", "k", "x", "y"))


def remote(src, dst, send, recv, to):
    return pltpu.make_async_remote_copy(
        src_ref=src, dst_ref=dst, send_sem=send, recv_sem=recv, device_id=to, device_id_type=MESH
    )


def hello(to):
    pl.semaphore_signal(pltpu.get_barrier_semaphore(), inc=1, device_id=to, device_id_type=MESH)


def meet(count):
    pl.semaphore_wait(pltpu.get_barrier_semaphore(), count)


def dot(a, b):
    return jnp.dot(a, b, precision=HI, preferred_element_type=F32)


def selection(meta):
    row = lax.broadcasted_iota(jnp.int32, (NB * G, TD * G), 0)
    lane = lax.broadcasted_iota(jnp.int32, (NB * G, TD * G), 1)
    first = meta[0:1, :].astype(jnp.int32)
    second = meta[1:2, :].astype(jnp.int32)
    flip = meta[2:3, :]
    bucket = row >> 3
    value = jnp.where(bucket == first, 1.0, 0.0) + jnp.where(bucket == second, flip, 0.0)
    return jnp.where((row & 7) == (lane & 7), value, 0.0).astype(BF16)


NBK = 64


def invert_block(block):
    n = NBK
    ident = (lax.broadcasted_iota(jnp.int32, (n, n), 0) == lax.broadcasted_iota(jnp.int32, (n, n), 1)).astype(F32)
    aug = jnp.concatenate([block, ident], axis=1)
    groups = n // G
    rows = [aug[g * G : (g + 1) * G, :] for g in range(groups)]
    sub = lax.broadcasted_iota(jnp.int32, (G, 2 * n), 0)
    for g in range(groups):
        cols = [
            {h: jnp.broadcast_to(rows[h][:, g * G + i : g * G + i + 1], (G, 2 * n)) for h in range(g, groups)}
            for i in range(G)
        ]
        scale = jnp.zeros((G, 2 * n), F32)
        for i in range(G):
            pivot = jnp.broadcast_to(cols[i][g][i : i + 1, :], (G, 2 * n))
            inv = 1.0 / pivot
            scale = jnp.where(sub == i, lax.rsqrt(pivot), scale)
            below = dict(cols[i])
            below[g] = jnp.where(sub > i, below[g], 0.0)
            for m in range(i + 1, G):
                f = jnp.broadcast_to(cols[m][g][i : i + 1, :], (G, 2 * n)) * inv
                for h in range(g, groups):
                    cols[m][h] = cols[m][h] - below[h] * f
            u = jnp.broadcast_to(rows[g][i : i + 1, :], (G, 2 * n)) * inv
            for h in range(g, groups):
                rows[h] = rows[h] - below[h] * u
        rows[g] = rows[g] * scale
    done = jnp.concatenate(rows, axis=0)
    return done[:, n:]


def start_factor(gram, work):
    work[:, :PS] = gram
    work[:, PS:] = (
        lax.broadcasted_iota(jnp.int32, (PS, PS), 0) == lax.broadcasted_iota(jnp.int32, (PS, PS), 1)
    ).astype(F32)


def factor_step(work, p):
    lo, hi = p * NBK, (p + 1) * NBK
    inv = invert_block(work[lo:hi, lo:hi])
    left, right = lo // HALF * HALF, PS + -(-hi // HALF) * HALF
    row = dot(inv, work[lo:hi, left:right])
    work[lo:hi, left:right] = row
    if hi < PS:
        work[hi:, left:right] = work[hi:, left:right] - dot(row[:, hi - left : PS - left].T, row)


VM = pl.BlockSpec(memory_space=pltpu.VMEM)
ANY = pl.BlockSpec(memory_space=pl.ANY)
DMA = pltpu.SemaphoreType.DMA
STEP_TILES = 8
QUARTER = PS // 4
OWN_ROWS = NB * G // NZ
TINY = 1e-30
FULL = 32767.0
FAR_FIRST = sorted(range(1, NZ), key=lambda d: -min(d, NZ - d))
RELAYS = ((4, (8, 5, 7)), (12, (14, 13, 15)), (1, (10, 9, 2)), (3, (6, 11)))


def to_code(value):
    return jnp.floor(value + 0.5).astype(jnp.int32).astype(jnp.int16)


def from_code(code):
    return code.astype(jnp.int32).astype(F32)


def top_of(value):
    return jnp.maximum(jnp.max(jnp.abs(value), axis=0, keepdims=True), TINY)


def mix_tiles(which, seeds, mat, mixers, m_ref, part):
    lane = lax.broadcasted_iota(jnp.int32, (1, TILE), 1) * 40503

    def some(step, carry):
        for pair in range(STEP_TILES // 2):
            parts = []
            for q in range(2):
                tile = step * STEP_TILES + 2 * pair + q
                hashed = (seeds[tile] ^ lane) * 69069
                sign = (1 - 2 * ((hashed >> 16) & 1)).astype(F32)
                mixer = mixers[which[tile]] * sign
                block = mat[pl.ds(pl.multiple_of(tile * TILE, TILE), TILE), :]
                parts.append(dot(mixer, block).reshape(TILE // G, G, mat.shape[1]))
            at = pl.multiple_of((step * STEP_TILES + 2 * pair) * G, 2 * G)
            m_ref[:, pl.ds(at, 2 * G), :] = jnp.concatenate(parts, axis=1).astype(BF16)
        return carry

    steps = TD // STEP_TILES // 2
    lax.fori_loop(part * steps, (part + 1) * steps, some, 0)


def fill_meta(seeds, pairs, meta_ref):
    tiles = lax.broadcasted_iota(jnp.int32, (1, TD * G), 1) // G
    first = jnp.zeros((1, TD * G), jnp.int32)
    second, seed = first, first
    for t in range(TD):
        first = jnp.where(tiles == t, pairs[0, t], first)
        second = jnp.where(tiles == t, pairs[1, t], second)
        seed = jnp.where(tiles == t, seeds[t], seed)
    flip = 1 - 2 * (seed >> 29 & 1)
    row = lax.broadcasted_iota(jnp.int32, (G, TD * G), 0)
    meta_ref[...] = jnp.where(row == 0, first, jnp.where(row == 1, second, flip)).astype(F32)


def main_kernel(
    which_in, seeds_in, pairs_in, mat_in, mixers_in, o_ref,
    which, seeds, pairs, mat, mixers, in_sems,
    m_ref, meta_ref, other_ref, x_ref, relay, y_ref, yq_ref, ys_ref, got_y, pq_ref, ps_ref,
    top_ref, got_t, w_ref, all_ref, g_ref, got_g, gram_ref, work, value, summed, pair, got_v,
    meta_sems, send_x, recv_x, send_r, recv_r,
    send_a, recv_a, send_b, recv_b, send_c, recv_c,
    send_as, recv_as, send_bs, recv_bs, send_t, recv_t,
    send_w, recv_w, send_g, recv_g, send_h, recv_h,
    pair_sems, send_v, recv_v,
):
    z, k, x, y = place()
    col = x * NX + y
    source = col == 0
    sibling = {"k": 1 - k}

    def plane(d):
        other = lax.rem(k * NC + col + d, NK * NC)
        c = lax.rem(other, NC)
        return other // NC, c, {"k": other // NC, "x": c // NX, "y": lax.rem(c, NX)}

    def up(d):
        return lax.rem(z + d, NZ)

    rows = TD * TILE // 2
    loads = [
        pltpu.make_async_copy(src, dst, in_sems.at[i])
        for i, (src, dst) in enumerate(
            (
                (which_in, which),
                (seeds_in, seeds),
                (pairs_in, pairs),
                (mixers_in, mixers),
                (mat_in.at[:rows, :], mat.at[:rows, :]),
                (mat_in.at[rows:, :], mat.at[rows:, :]),
            )
        )
    ]
    for load in loads:
        load.start()
    for d in FAR_FIRST:
        hello({"z": up(d)})
    for d in range(1, NK * NC):
        hello(plane(d)[2])
    for load in loads[:-1]:
        load.wait()
    mix_tiles(which, seeds, mat, mixers, m_ref, 0)
    fill_meta(seeds, pairs, meta_ref)
    meet(NK * NC - 1 + NZ - 1)

    sent = []

    def go(copy):
        copy.start()
        sent.append(copy)

    def landed(ref, recv):
        remote(ref, ref, send_x.at[0, 0, 0], recv, sibling).wait_recv()

    part_rows = TD * G // 2

    def rows_in(part):
        return pl.ds(part * part_rows, part_rows)

    def half(c, kd, part):
        return m_ref.at[c, rows_in(part), kd * HALF : (kd + 1) * HALF]

    def home(part):
        return x_ref.at[k, rows_in(part), :]

    def spot(c):
        return {"x": c // NX, "y": c % NX}

    pieces = ([], [])
    for part in range(2):
        for j in range(3):
            for first, rest in RELAYS:
                if j < len(rest):
                    for kd in range(NK):
                        c = rest[j]
                        pieces[part].append(
                            (half(c, kd, part), relay.at[j, kd, rows_in(part), :], send_x.at[c, kd, part],
                             recv_r.at[j, kd, part], spot(first))
                        )
        for first, rest in RELAYS:
            for kd in range(NK):
                pieces[part].append(
                    (half(first, kd, part), home(part), send_x.at[first, kd, part], recv_x.at[k, part],
                     {"k": kd, **spot(first)})
                )
        cross_half = m_ref.at[0, rows_in(part), pl.ds(pl.multiple_of((1 - k) * HALF, HALF), HALF)]
        pieces[part].append((cross_half, home(part), send_x.at[0, 0, part], recv_x.at[k, part], sibling))

    @pl.when(source)
    def _():
        for piece in pieces[0]:
            remote(*piece).start()

    go(remote(meta_ref, other_ref, meta_sems.at[0], meta_sems.at[1], sibling))
    loads[-1].wait()
    mix_tiles(which, seeds, mat, mixers, m_ref, 1)

    @pl.when(source)
    def _():
        for piece in pieces[1]:
            remote(*piece).start()
        x_ref[k] = jnp.where(k == 0, m_ref[0, :, :HALF], m_ref[0, :, HALF:])

    def onward(j, kd, part, c):
        return remote(
            relay.at[j, kd, rows_in(part), :], home(part), send_r.at[j, kd, part], recv_x.at[k, part],
            {"k": kd, **spot(c)}
        )

    for first, rest in RELAYS:
        @pl.when(col == first)
        def _():
            for part in range(2):
                for j, c in enumerate(rest):
                    for kd in range(NK):
                        landed(relay.at[j, kd, rows_in(part), :], recv_r.at[j, kd, part])
                        onward(j, kd, part, c).start()

    landed(other_ref, meta_sems.at[1])
    mine = selection(meta_ref[...])
    theirs = selection(other_ref[...])

    part = jnp.zeros((NB * G, HALF), F32)
    for p in range(2):
        @pl.when(jnp.logical_not(source))
        def _():
            landed(x_ref.at[k, rows_in(p), :], recv_x.at[k, p])

        landed(x_ref.at[1 - k, rows_in(p), :], recv_x.at[1 - k, p])
        span = slice(p * part_rows, (p + 1) * part_rows)
        part = part + jnp.dot(mine[:, span], x_ref[k, span, :], preferred_element_type=F32)
        part = part + jnp.dot(theirs[:, span], x_ref[1 - k, span, :], preferred_element_type=F32)
    y_ref[...] = part.reshape(y_ref.shape)
    top = top_of(part)
    yq_ref[...] = to_code(part * (FULL / top)).reshape(yq_ref.shape)
    ys_ref[z] = top

    for d in FAR_FIRST:
        go(remote(yq_ref.at[up(d)], got_y.at[d - 1], send_a.at[d - 1], recv_a.at[d - 1], {"z": up(d)}))
        go(remote(ys_ref.at[z], ys_ref.at[z], send_as.at[d - 1], recv_as.at[d - 1], {"z": up(d)}))
    acc = y_ref[z]
    for d in FAR_FIRST[::-1]:
        zs = up(NZ - d)
        landed(got_y.at[d - 1], recv_a.at[d - 1])
        landed(ys_ref.at[zs], recv_as.at[d - 1])
        acc = acc + from_code(got_y[d - 1]) * (ys_ref[zs] * (1.0 / FULL))
    top = ys_ref[0]
    for other_z in range(1, NZ):
        top = top + ys_ref[other_z]
    top = top * 1.00001
    pq_ref[k, z] = to_code(acc * (FULL / top))
    ps_ref[k] = top * (1.0 / FULL)
    go(remote(ps_ref.at[k], ps_ref.at[k], send_bs, recv_bs, sibling))

    for d in FAR_FIRST:
        go(remote(pq_ref.at[k, z], pq_ref.at[k, z], send_b.at[d - 1], recv_b.at[d - 1], {"z": up(d)}))
    go(remote(pq_ref.at[k, z], pq_ref.at[k, z], send_c.at[0], recv_c.at[0], sibling))
    for d in FAR_FIRST[::-1]:
        zs = up(NZ - d)
        landed(pq_ref.at[k, zs], recv_b.at[d - 1])
        go(remote(pq_ref.at[k, zs], pq_ref.at[k, zs], send_c.at[d], recv_c.at[d], sibling))
    landed(ps_ref.at[1 - k], recv_bs)
    for d in [0] + FAR_FIRST[::-1]:
        landed(pq_ref.at[1 - k, up(NZ - d)], recv_c.at[d])

    sketch = jnp.concatenate(
        [from_code(pq_ref[kk]).reshape(NB * G, HALF) * ps_ref[kk] for kk in range(NK)], axis=1
    )
    top_ref[...] = top_of(sketch)

    def same_core(d):
        c = lax.rem(col + d, NC)
        return {"x": c // NX, "y": lax.rem(c, NX)}

    for d in range(1, NC):
        go(remote(top_ref, got_t.at[d - 1], send_t.at[d - 1], recv_t.at[d - 1], same_core(d)))
    turned = sketch.T
    g_ref[...] = dot(turned, sketch)

    def rows_of(kk, c):
        return pl.ds(pl.multiple_of(kk * HALF + c * G, G), G)

    for d in range(1, NC):
        go(remote(g_ref.at[rows_of(k, lax.rem(col + d, NC)), :], got_g.at[d - 1], send_g.at[d - 1], recv_g.at[d - 1], same_core(d)))
    high = turned.astype(BF16)
    rest = turned - high.astype(F32)
    low = rest.astype(BF16)
    last = (rest - low.astype(F32)).astype(BF16)
    weight = sum(jnp.dot(piece, mine, preferred_element_type=F32) for piece in (last, low, high))
    top = top_ref[...]
    for d in range(1, NC):
        landed(got_t.at[d - 1], recv_t.at[d - 1])
        top = jnp.maximum(top, got_t[d - 1])
    unit = top * (2.0 / (FULL - 1.0))
    inverse = jnp.broadcast_to(1.0 / unit, (G, PS)).T[:, 0:1]
    w_ref[...] = to_code(weight * inverse)

    def piece_of(h, s):
        return pl.ds((2 * h + s) * QUARTER, QUARTER)

    def index(h, a, b):
        if h == 0:
            return lax.rem(x + a, NX) * NX + lax.rem(y + b, NX)
        return lax.rem(x + b, NX) * NX + lax.rem(y + a, NX)

    def send(h, a, b, s, stage, direction):
        c = index(h, a, b)
        there = all_ref.at[c, piece_of(h, s), :]
        here = w_ref.at[piece_of(h, s), :] if a == b == 0 else there
        step = 1 if direction == 0 else NX - 1
        to = {"x": lax.rem(x + step, NX)} if (h == 0) == (stage == 0) else {"y": lax.rem(y + step, NX)}
        go(remote(here, there, send_w.at[h, c, s, stage, direction], recv_w.at[h, c, s], to))

    seen = {(h, 0, 0, s) for h in range(2) for s in range(2)}

    def arrived(h, a, b, s):
        if (h, a, b, s) not in seen:
            seen.add((h, a, b, s))
            c = index(h, a, b)
            landed(all_ref.at[c, piece_of(h, s), :], recv_w.at[h, c, s])

    def across(h, a, s):
        arrived(h, a, 0, s)
        send(h, a, 0, s, 1, s)
        send(h, a, 0, s, 1, 1 - s)

    def pass_on(a):
        for h in range(2):
            arrived(h, a, 3, 0)
            send(h, a, 3, 0, 1, 0)
            arrived(h, a, 1, 1)
            send(h, a, 1, 1, 1, 1)

    def own_blocks(stage):
        for turn in range(2):
            for s in range(2):
                for h in range(2):
                    send(h, 0, 0, s, stage, s if turn == 0 else 1 - s)

    own_blocks(0)
    acc = g_ref[rows_of(k, col), :]
    for d in range(1, NC):
        landed(got_g.at[d - 1], recv_g.at[d - 1])
        acc = acc + got_g[d - 1]
    gram_ref[rows_of(k, col), :] = acc
    for d in range(1, NK * NC):
        own = gram_ref.at[rows_of(k, col), :]
        go(remote(own, own, send_h.at[d - 1], recv_h.at[d - 1], plane(d)[2]))
    own_blocks(1)

    for h in range(2):
        arrived(h, 3, 0, 0)
        send(h, 3, 0, 0, 0, 0)
        arrived(h, 1, 0, 1)
        send(h, 1, 0, 1, 0, 1)
    for a, s in ((3, 0), (1, 1), (3, 1), (1, 0)):
        for h in range(2):
            across(h, a, s)
    pass_on(0)
    for d in range(1, NK * NC):
        kk, c, _ = plane(NK * NC - d)
        landed(gram_ref.at[rows_of(kk, c), :], recv_h.at[d - 1])
    all_ref[col] = w_ref[...]
    start_factor(gram_ref[...], work)
    factor_step(work, 0)
    for h in range(2):
        for s in range(2):
            across(h, 2, s)
    pass_on(3)
    factor_step(work, 1)
    pass_on(1)
    factor_step(work, 2)
    pass_on(2)
    factor_step(work, 3)

    def ready(dx, dy):
        for s in range(2):
            arrived(0, dx, dy, s)
            arrived(1, dy, dx, s)

    def add(dx, dy, acc):
        c = lax.rem(x + dx, NX) * NX + lax.rem(y + dy, NX)
        w = from_code(all_ref[c])
        high = w.astype(BF16)
        low = (w - high.astype(F32)).astype(BF16)
        tiles = m_ref[c]
        for part in (high, low):
            acc = acc + jnp.dot(part, tiles, preferred_element_type=F32)
        return acc

    cross = jnp.zeros((PS, m_ref.shape[2]), F32)
    for d in range(NX):
        ready(d, 0)
        ready(0, d)
    cross = lax.fori_loop(
        0, 2 * NX - 1, lambda j, acc: add(jnp.where(j < NX, j, 0), jnp.where(j < NX, 0, j - NX + 1), acc), cross
    )
    for offsets in (((1, 1), (1, 3), (3, 1), (3, 3)), ((1, 2), (3, 2), (2, 1), (2, 3)), ((2, 2),)):
        for dx, dy in offsets:
            ready(dx, dy)
        for dx, dy in offsets:
            cross = add(dx, dy, cross)
    value[...] = dot(work[:, PS:] * unit, cross).reshape(value.shape)
    go(remote(value.at[:, 1 - k], pair, pair_sems.at[0], pair_sems.at[1], sibling))
    landed(pair, pair_sems.at[1])
    summed[...] = value[:, k] + pair[...]
    for d in FAR_FIRST:
        go(remote(summed.at[up(d)], got_v.at[d - 1], send_v.at[d - 1], recv_v.at[d - 1], {"z": up(d)}))
    acc = summed[z]
    for d in FAR_FIRST[::-1]:
        landed(got_v.at[d - 1], recv_v.at[d - 1])
        acc = acc + got_v[d - 1]
    o_ref[...] = acc

    @pl.when(source)
    def _():
        for piece in pieces[0] + pieces[1]:
            remote(*piece).wait_send()

    for first, rest in RELAYS:
        @pl.when(col == first)
        def _():
            for part in range(2):
                for j, c in enumerate(rest):
                    for kd in range(NK):
                        onward(j, kd, part, c).wait_send()

    for copy in sent:
        copy.wait_send()


def local(matrix, mixers, bucket_pair, mixer_index, sign_seed):
    width = matrix.shape[1]
    one, two, plane = (NZ - 1,), (2,), (NK * NC - 1,)
    return pl.pallas_call(
        main_kernel,
        out_shape=jax.ShapeDtypeStruct((G, width), F32),
        in_specs=[ANY] * 5,
        out_specs=VM,
        scratch_shapes=[
            pltpu.SMEM((TD,), jnp.int32),
            pltpu.SMEM((TD,), jnp.int32),
            pltpu.SMEM((2, TD), jnp.int32),
            pltpu.VMEM(matrix.shape, F32),
            pltpu.VMEM(mixers.shape, F32),
            DMA((6,)),
            pltpu.VMEM((NC, TD * G, width), BF16),
            pltpu.VMEM((G, TD * G), F32),
            pltpu.VMEM((G, TD * G), F32),
            pltpu.VMEM((NK, TD * G, HALF), BF16),
            pltpu.VMEM((3, NK, TD * G, HALF), BF16),
            pltpu.VMEM((NZ, OWN_ROWS, HALF), F32),
            pltpu.VMEM((NZ, OWN_ROWS, HALF), jnp.int16),
            pltpu.VMEM((NZ, 1, HALF), F32),
            pltpu.VMEM((NZ - 1, OWN_ROWS, HALF), jnp.int16),
            pltpu.VMEM((NK, NZ, OWN_ROWS, HALF), jnp.int16),
            pltpu.VMEM((NK, 1, HALF), F32),
            pltpu.VMEM((1, PS), F32),
            pltpu.VMEM((NC - 1, 1, PS), F32),
            pltpu.VMEM((PS, TD * G), jnp.int16),
            pltpu.VMEM((NC, PS, TD * G), jnp.int16),
            pltpu.VMEM((PS, PS), F32),
            pltpu.VMEM((NC - 1, G, PS), F32),
            pltpu.VMEM((PS, PS), F32),
            pltpu.VMEM((PS, 2 * PS), F32),
            pltpu.VMEM((NZ, NK, G, width), F32),
            pltpu.VMEM((NZ, G, width), F32),
            pltpu.VMEM((NZ, G, width), F32),
            pltpu.VMEM((NZ - 1, G, width), F32),
            DMA(two), DMA((NC, NK, 2)), DMA((NK, 2)), DMA((3, NK, 2)), DMA((3, NK, 2)),
            DMA(one), DMA(one), DMA(one), DMA(one), DMA((NZ,)), DMA((NZ,)),
            DMA(one), DMA(one), DMA, DMA, DMA((NC - 1,)), DMA((NC - 1,)),
            DMA((2, NC, 2, 2, 2)), DMA((2, NC, 2)), DMA((NC - 1,)), DMA((NC - 1,)), DMA(plane), DMA(plane),
            DMA(two), DMA(one), DMA(one),
        ],
        compiler_params=pltpu.CompilerParams(
            collective_id=1, has_side_effects=True
        ),
        name="main",
    )(mixer_index, sign_seed, bucket_pair.T, matrix, mixers)


def solution(mesh):
    split = Mesh(mesh.devices.reshape(NZ, NK, NX, NX), ("z", "k", "x", "y"))
    return jax.shard_map(
        local,
        mesh=split,
        in_specs=(P(ROWS, COLS), P(), P(ROWS, None), P(ROWS), P(ROWS)),
        out_specs=P(ROWS, COLS),
        check_vma=False,
    )
```
